768 devices in a mesh: dp: 48 (over z_lo, x, core), grp: 16 (over y, z_hi).
Axes of the slice: x: 4, y: 8, z: 12 (z_hi: 2, z_lo: 6; z = z_hi * 6 + z_lo), core: 2. Of those that a mesh axis runs over, the one named last changes fastest.
Arguments:
- embeddings: bfloat16 [294912, 512], P(('dp', 'grp')), may hold values from -0.31 to 0.31
- order: int32 [768, 384], P(('dp', 'grp')), may hold values from 0 to 383, as said below
Outputs:
- emb_grad: bfloat16 [294912, 512], P(('dp', 'grp'))
- row_loss: float32 [768, 384], P(('dp', 'grp'))
The draws below stay inside these ranges and needn't reach their ends.
Inputs may be any that keep to these rules, and one draw needn't show every extreme that they name: Each row of order is a permutation of 0 .. 383.
All inputs are finite; a program needn't handle non-finite values.
Results may differ from the reference program's by a relative error of at most 0.0046.
Values may be sent and summed in bfloat16 or wider, within the bound.
No kernel may reach another device: no remote copies, remote signals or barrier semaphores. Data moves between devices by JAX's collectives and lax.ppermute only.
A program may use at most 32 MiB of HBM per device.

```python
import math
import jax
import jax.numpy as jnp
from jax import lax

D = 512
K = 16
ROWS_DEV = 384
TOTAL = 294912
N_DP = 48
N_GRP = 16


entry_scale = 0.03


def slot_orders(key):
    owner_keys = jax.random.split(jax.random.fold_in(key, 11), N_DP * N_GRP)
    shuffled = jax.vmap(lambda owner_key: jax.random.permutation(owner_key, ROWS_DEV))(owner_keys)
    return shuffled.astype(jnp.int32)


def draw_order(key, part):
    return slot_orders(key)


def draw_embeddings(key, part):
    owners = N_DP * N_GRP
    per_peer = ROWS_DEV // N_DP
    class_count = ROWS_DEV // K
    slot_table = slot_orders(key)
    owner_index = jnp.arange(owners, dtype=jnp.int32)[:, None]
    slot_index = jnp.broadcast_to(jnp.arange(ROWS_DEV, dtype=jnp.int32)[None, :], (owners, ROWS_DEV))
    slot_of_row = jnp.zeros((owners, ROWS_DEV), jnp.int32).at[owner_index, slot_table].set(slot_index)
    class_of_row = slot_of_row // K
    family_row = owner_index // N_GRP * ROWS_DEV + slot_of_row
    block_row = owner_index * class_count + class_of_row
    family_key = jax.random.fold_in(key, 21)
    block_key = jax.random.fold_in(key, 22)
    noise_key = jax.random.fold_in(key, 23)
    ratio_key = jax.random.fold_in(key, 24)
    family = jax.random.truncated_normal(family_key, -4.0, 4.0, (N_DP * ROWS_DEV, D), jnp.float32)
    blocks = jax.random.truncated_normal(block_key, -4.0, 4.0, (owners * class_count, D), jnp.float32)
    noise = jax.random.truncated_normal(noise_key, -4.0, 4.0, (owners, ROWS_DEV, D), jnp.float32)
    ratio_sq = jnp.exp(jax.random.uniform(ratio_key, (owners, ROWS_DEV), jnp.float32, math.log(0.08), math.log(1.2)))
    shared = 0.5
    centre = math.sqrt(shared) * family[family_row] + math.sqrt(1.0 - shared) * blocks[block_row]
    arrived = entry_scale * (centre + jnp.sqrt(ratio_sq)[:, :, None] * noise)
    sampler = arrived.reshape(N_DP, N_GRP, N_DP, per_peer, D).transpose(2, 1, 0, 3, 4)
    return sampler.reshape(owners * ROWS_DEV, D).astype(jnp.bfloat16)


def setup_inputs(seed: int = 0) -> dict:
    keys = jax.random.split(jax.random.key(seed), 3)
    embeddings = draw_embeddings(jax.random.fold_in(keys[2], 71), 0)
    order = draw_order(jax.random.fold_in(keys[2], 71), 0)
    return {"embeddings": embeddings, "order": order}


gamma = 16.0
matching_offsets = (1, 2, 3)

def device_step(unit_rows, partner_rows):
    row_count = unit_rows.shape[0]
    own_sim = jnp.dot(unit_rows, unit_rows.T, preferred_element_type=jnp.float32)
    classes = jnp.arange(row_count, dtype=jnp.int32) // K
    same_class = classes[:, None] == classes[None, :]
    diagonal = jnp.arange(row_count)[:, None] == jnp.arange(row_count)[None, :]
    positive = jnp.logical_and(same_class, jnp.logical_not(diagonal))
    negative = jnp.logical_not(same_class)
    pos_exp = jnp.where(positive, jnp.exp(-gamma * own_sim), jnp.float32(0.0))
    neg_exp = jnp.where(negative, jnp.exp(gamma * own_sim), jnp.float32(0.0))
    pos_sum = lax.optimization_barrier(jnp.sum(pos_exp, axis=1))
    neg_sum = lax.optimization_barrier(jnp.sum(neg_exp, axis=1))
    cross_exps = []
    for index in range(3):
        cross = jnp.dot(unit_rows, partner_rows[index].T, preferred_element_type=jnp.float32)
        cross_exp = jnp.exp(gamma * cross)
        neg_sum = neg_sum + lax.optimization_barrier(jnp.sum(cross_exp, axis=1))
        cross_exps.append(cross_exp)
    product = pos_sum * neg_sum
    row_loss = jnp.log(1.0 + product)
    weight = product / (1.0 + product)
    coef_own = (weight[:, None] * gamma * (neg_exp / neg_sum[:, None] - pos_exp / pos_sum[:, None])).astype(jnp.bfloat16)
    own_grad = jnp.dot(coef_own, unit_rows, preferred_element_type=jnp.float32)
    own_grad = own_grad + jnp.dot(coef_own.T, unit_rows, preferred_element_type=jnp.float32)
    partials = []
    for index in range(3):
        coef_cross = (weight[:, None] * gamma * cross_exps[index] / neg_sum[:, None]).astype(jnp.bfloat16)
        own_grad = own_grad + jnp.dot(coef_cross, partner_rows[index], preferred_element_type=jnp.float32)
        partials.append(jnp.dot(coef_cross.T, unit_rows, preferred_element_type=jnp.float32).astype(jnp.bfloat16))
    return (row_loss, own_grad, jnp.stack(partials, axis=0))

def reference(embeddings, order):
    devices_all = N_DP * N_GRP
    per_peer = ROWS_DEV // N_DP
    arrived = embeddings.reshape(N_DP, N_GRP, N_DP, per_peer, D).transpose(2, 1, 0, 3, 4).reshape(devices_all, ROWS_DEV, D)
    owned = jnp.take_along_axis(arrived, order[:, :, None].astype(jnp.int32), axis=1)
    owned_f = owned.astype(jnp.float32)
    inv_norm = lax.rsqrt(lax.optimization_barrier(jnp.sum(owned_f * owned_f, axis=2, keepdims=True)) + 1e-06)
    unit_f = owned_f * inv_norm
    unit_rows = unit_f.astype(jnp.bfloat16)
    unit_grid = unit_rows.reshape(N_DP, N_GRP, ROWS_DEV, D)
    partners = jnp.stack([jnp.roll(unit_grid, offset, axis=1) for offset in matching_offsets], axis=2)
    partners = partners.reshape(devices_all, 3, ROWS_DEV, D)
    row_loss, own_grad, partials = lax.map(lambda pair: device_step(pair[0], pair[1]), (unit_rows, partners))
    partials = partials.reshape(N_DP, N_GRP, 3, ROWS_DEV, D)
    unit_grad = own_grad.reshape(N_DP, N_GRP, ROWS_DEV, D)
    for index in range(3):
        unit_grad = unit_grad + jnp.roll(partials[:, :, index], -matching_offsets[index], axis=1).astype(jnp.float32)
    unit_grad = unit_grad.reshape(devices_all, ROWS_DEV, D)
    owned_grad = ((unit_grad - unit_f * lax.optimization_barrier(jnp.sum(unit_f * unit_grad, axis=2, keepdims=True))) * inv_norm).astype(jnp.bfloat16)

    def place_back(grad_rows, slots):
        return jnp.zeros_like(grad_rows).at[slots].set(grad_rows)
    arrival_grad = jax.vmap(place_back)(owned_grad, order.astype(jnp.int32))
    emb_grad = arrival_grad.reshape(N_DP, N_GRP, N_DP, per_peer, D).transpose(2, 1, 0, 3, 4).reshape(TOTAL, D)
    return (emb_grad, row_loss)
```

```python
import functools

import jax
import jax.numpy as jnp
import numpy as np
from jax import lax
from jax.experimental import pallas as pl
from jax.experimental.pallas import tpu as pltpu
from jax.sharding import Mesh
from jax.sharding import PartitionSpec as P

K = 16
gamma = 16.0
F32 = jnp.float32
BF16 = jnp.bfloat16
WHERE = ("zl", "x", "zh")


def rows_by_rows(a, b):
    return lax.dot_general(a, b, (((1,), (1,)), ((), ())), preferred_element_type=F32)


def cols_by_cols(a, b):
    return lax.dot_general(a, b, (((0,), (0,)), ((), ())), preferred_element_type=F32)


def row_ids(half, core, shape, axis):
    i = lax.broadcasted_iota(jnp.int32, shape, axis)
    return (i // 8) * 16 + core * 8 + i % 8


def pick_orders(core, mine, other):
    first = core == 0
    return jnp.where(first, mine, other), jnp.where(first, other, mine)


def pack_kernel(core_ref, x_ref, mine_ref, other_ref, full_ref, a_ref, b_ref):
    core = core_ref[0]
    half = a_ref.shape[0] - 8
    rows = mine_ref.shape[1]
    features = x_ref.shape[-1]
    slot_class = (lax.broadcasted_iota(jnp.int32, (8, rows), 1) // K).astype(BF16)
    orders = pick_orders(core, mine_ref[...], other_ref[...])
    ids = row_ids(half, core, (half, rows), 0)
    labels = []
    for order in orders:
        chosen = jnp.where(ids == order, 1.0, 0.0).astype(BF16)
        labels.append(rows_by_rows(slot_class, chosen))
    tile = jnp.zeros((8, features), F32)
    room = features // 2
    gap = jnp.zeros((8, room - half), F32)
    tile = jnp.concatenate([labels[0], gap, labels[1], gap], axis=1).astype(BF16)
    for which in range(2):
        x = x_ref[:, which].astype(F32).reshape(half, features)
        inv = lax.rsqrt(jnp.sum(x * x, axis=1, keepdims=True) + 1e-06)
        unit = (x * inv).astype(BF16)
        if which == 0:
            full_ref[0:half] = unit
            a_ref[0:half] = unit
        else:
            full_ref[half + 8 :] = unit
            b_ref[...] = unit
    full_ref[half : half + 8] = tile
    a_ref[half : half + 8] = tile


def loss_kernel(
    core_ref, x_ref, mine_ref, other_ref,
    y0_ref, y0o_ref, dn_ref, dno_ref, up_ref, upo_ref, dn2_ref, dn2o_ref, up2_ref, up2o_ref,
    grad_ref, loss_ref, w, coef_rows, coef_cols,
):
    core = core_ref[0]
    half = dn2_ref.shape[0]
    rows = 2 * half
    features = x_ref.shape[-1]
    room = features // 2
    second = half + 8

    def place(block, own, other, start):
        w[block * rows : block * rows + half] = own[start : start + half]
        w[block * rows + half : (block + 1) * rows] = other[start : start + half]

    place(0, dn2_ref, dn2o_ref, 0)
    place(1, dn_ref, dno_ref, 0)
    place(2, dn_ref, dno_ref, second)
    place(3, y0_ref, y0o_ref, 0)
    place(4, y0_ref, y0o_ref, second)
    place(5, up_ref, upo_ref, 0)
    place(6, up_ref, upo_ref, second)
    place(7, up2_ref, up2o_ref, 0)

    def labels_of(own, other, which):
        lanes = slice(which * room, which * room + half)
        return jnp.concatenate(
            [own[half:second, lanes].astype(F32), other[half:second, lanes].astype(F32)], axis=1
        )[0:1]

    label_rows = {
        3: labels_of(y0_ref, y0o_ref, 0),
        4: labels_of(y0_ref, y0o_ref, 1),
        5: labels_of(up_ref, upo_ref, 0),
        6: labels_of(up_ref, upo_ref, 1),
        7: labels_of(up2_ref, up2o_ref, 0),
    }
    kinds = -(-(rows // K) // 16) * 16
    kind = lax.broadcasted_iota(jnp.int32, (kinds, rows), 0).astype(F32)
    diagonal = lax.broadcasted_iota(jnp.int32, (rows, rows), 0) == lax.broadcasted_iota(
        jnp.int32, (rows, rows), 1
    )
    losses = []
    for i in range(3, 8):
        anchor = w[i * rows : (i + 1) * rows]
        one_hot = jnp.where(kind == label_rows[i], 1.0, 0.0).astype(BF16)
        same = cols_by_cols(one_hot, one_hot) > 0.5
        own = rows_by_rows(anchor, anchor)
        e_own = jnp.exp(gamma * jnp.where(same, -own, own))
        pos = jnp.where(jnp.logical_and(same, jnp.logical_not(diagonal)), e_own, 0.0)
        neg = jnp.where(same, 0.0, e_own)
        pos_sum = jnp.sum(pos, axis=1, keepdims=True)
        neg_sum = jnp.sum(neg, axis=1, keepdims=True)
        cross = jnp.exp(gamma * rows_by_rows(anchor, w[(i - 3) * rows : i * rows]))
        neg_sum = neg_sum + jnp.sum(cross, axis=1, keepdims=True)
        product = pos_sum * neg_sum
        weight = product / (1.0 + product)
        on_neg = gamma * weight / neg_sum
        on_pos = gamma * weight / pos_sum
        coef_own = (on_neg * neg - on_pos * pos).astype(BF16)
        if i < 5:
            losses.append(jnp.log(1.0 + product))
            mine = i - 3
            coef_rows[mine, :, 0 : 3 * rows] = (on_neg[0:half] * cross[0:half]).astype(BF16)
            coef_rows[mine, :, 3 * rows :] = coef_own[0:half]
        for target in (3, 4):
            if target == i:
                part = coef_own[:, 0:half]
            elif i - 3 <= target < i:
                lane = (target - (i - 3)) * rows
                part = (on_neg * cross[:, lane : lane + half]).astype(BF16)
            else:
                continue
            first = (i - target) * rows
            coef_cols[target - 3, first : first + rows] = part

    for which in range(2):
        total = jnp.dot(
            coef_rows[which], w[which * rows : (which + 4) * rows], preferred_element_type=F32
        )
        total = total + cols_by_cols(
            coef_cols[which], w[(which + 3) * rows : (which + 7) * rows]
        )
        x = x_ref[:, which].astype(F32).reshape(half, features)
        inv = lax.rsqrt(jnp.sum(x * x, axis=1, keepdims=True) + 1e-06)
        u = x * inv
        grad = (total - u * jnp.sum(u * total, axis=1, keepdims=True)) * inv
        grad_ref[:, which] = grad.reshape(half // 8, 8, features).astype(BF16)

    ids = jnp.concatenate(
        [row_ids(half, core, (half, rows), 0), row_ids(half, 1 - core, (half, rows), 0)], axis=0
    )
    orders = pick_orders(core, mine_ref[...], other_ref[...])
    by_slot = [
        jnp.sum(jnp.where(ids == order, loss, 0.0), axis=0, keepdims=True)
        for order, loss in zip(orders, losses)
    ]
    loss_ref[...] = jnp.where(core == 0, by_slot[0], by_slot[1])


VMEM = pl.BlockSpec(memory_space=pltpu.VMEM)
SMEM = pl.BlockSpec(memory_space=pltpu.SMEM)


def on_device(embeddings, order):
    rows, features = embeddings.shape
    peers = lax.axis_size(WHERE)
    per_peer = rows // peers
    half = rows // 2
    core = lax.axis_index("c").astype(jnp.int32).reshape(1)
    ring = lax.axis_size("y")

    turned = [(c * 2 + h, h * 2 + c) for h in range(2) for c in range(2)]
    crossed = [(c * 2 + h, (1 - h) * 2 + c) for h in range(2) for c in range(2)]
    mine = lax.ppermute(order, ("c", "zh"), turned)
    other = lax.ppermute(order, ("c", "zh"), crossed)

    def swap_cores(value):
        return lax.ppermute(value, "c", [(0, 1), (1, 0)])

    def along(value, distance):
        return lax.ppermute(value, "y", [(i, (i + distance) % ring) for i in range(ring)])

    arrived = lax.all_to_all(
        embeddings.reshape(peers, per_peer, features), WHERE, 0, 0, tiled=True
    ).reshape(peers // 2, 2, per_peer, features)

    full, part_a, part_b = pl.pallas_call(
        pack_kernel,
        out_shape=(
            jax.ShapeDtypeStruct((rows + 8, features), BF16),
            jax.ShapeDtypeStruct((half + 8, features), BF16),
            jax.ShapeDtypeStruct((half, features), BF16),
        ),
        in_specs=[SMEM, VMEM, VMEM, VMEM],
        out_specs=(VMEM, VMEM, VMEM),
        name="pack",
        cost_estimate=pl.CostEstimate(flops=10**7, bytes_accessed=10**6, transcendentals=0),
    )(core, arrived, mine, other)

    down = along(full, 1)
    up = along(full, -1)
    down2 = along(part_b, 2)
    up2 = along(part_a, -2)
    full_o = swap_cores(full)
    down_o = swap_cores(down)
    up_o = swap_cores(up)
    down2_o = swap_cores(down2)
    up2_o = swap_cores(up2)

    grad, loss = pl.pallas_call(
        loss_kernel,
        out_shape=(
            jax.ShapeDtypeStruct((peers // 2, 2, per_peer, features), BF16),
            jax.ShapeDtypeStruct((1, rows), F32),
        ),
        in_specs=[SMEM] + [VMEM] * 13,
        out_specs=(VMEM, VMEM),
        scratch_shapes=[
            pltpu.VMEM((8 * rows, features), BF16),
            pltpu.VMEM((2, half, 4 * rows), BF16),
            pltpu.VMEM((2, 4 * rows, half), BF16),
        ],
        name="loss_and_grad",
        cost_estimate=pl.CostEstimate(
            flops=4 * 10**9, bytes_accessed=10**7, transcendentals=3 * 10**6
        ),
    )(
        core, arrived, mine, other, full, full_o, down, down_o, up, up_o, down2, down2_o, up2, up2_o
    )

    row_loss = lax.ppermute(loss, ("c", "zh"), turned)
    sent_back = lax.all_to_all(
        grad.reshape(peers, per_peer, features), WHERE, 0, 0, tiled=True
    )
    return sent_back.reshape(rows, features), row_loss


def solution(mesh):
    dp, grp = mesh.devices.shape
    zl, x = SPLIT.get((dp, grp), (6, 4))
    parts = Mesh(
        mesh.devices.reshape(zl, x, 2, grp // 2, 2), ("zl", "x", "c", "y", "zh")
    )
    placed = P(("zl", "x", "c", "y", "zh"), None)
    return jax.shard_map(
        on_device, mesh=parts, in_specs=(placed, placed), out_specs=(placed, placed), check_vma=False
    )


SPLIT = {(48, 16): (6, 4)}
```

```python
import jax
import jax.numpy as jnp
from jax import lax
from jax.experimental import pallas as pl
from jax.experimental.pallas import tpu as pltpu
from jax.sharding import Mesh
from jax.sharding import PartitionSpec as P


K = 16
gamma = 16.0
F32 = jnp.float32
BF16 = jnp.bfloat16
WHERE = ("zl", "x", "zh")
LIMIT = 20 * 2**20


def rows_by_rows(a, b):
    return lax.dot_general(a, b, (((1,), (1,)), ((), ())), preferred_element_type=F32)


def block_ids(rows, core, shape, axis):
    half = rows // 2
    i = lax.broadcasted_iota(jnp.int32, shape, axis)
    source = jnp.where(i < half, core, 1 - core)
    i = jnp.where(i < half, i, i - half)
    return (i // 8) * 16 + source * 8 + i % 8


def chip_rows(own, sib):
    half = own.shape[0] // 2
    return jnp.concatenate([own[0:half], sib[0:half], own[half:], sib[half:]], axis=0)


def as_row(column):
    return jnp.broadcast_to(column, (column.shape[0], 128)).T[0:1]


def mask_kernel(core_ref, oa_ref, ob_ref, sign_ref):
    core = core_ref[0]

    @pl.when(core == 0)
    def _():
        rows = oa_ref.shape[1]
        ids = block_ids(rows, core, (rows, rows), 0)
        slot = lax.broadcasted_iota(jnp.int32, (rows, 128), 0) // K
        kind = lax.broadcasted_iota(jnp.int32, (rows, 128), 1)
        hot = []
        for which, ref in enumerate((oa_ref, ob_ref)):
            chosen = jnp.where(ids == ref[...], 1.0, 0.0).astype(BF16)
            table = jnp.where(kind == slot + which * (rows // K), 1.0, 0.0).astype(BF16)
            hot.append(jnp.dot(chosen, table, preferred_element_type=F32).astype(BF16))
        hot = jnp.concatenate(hot, axis=0)
        same = rows_by_rows(hot, hot)
        shape = (2 * rows, 2 * rows)
        diagonal = lax.broadcasted_iota(jnp.int32, shape, 0) == lax.broadcasted_iota(
            jnp.int32, shape, 1
        )
        sign_ref[...] = jnp.where(diagonal, 0.0, 1.0 - 2.0 * same)


def pack_kernel(core_ref, x_ref, full_ref, near_ref, far_ref):
    core = core_ref[0]
    half = near_ref.shape[0]
    units = []
    for which in range(2):
        x = x_ref[:, which].astype(F32).reshape(half, x_ref.shape[-1])
        inv = lax.rsqrt(jnp.sum(x * x, axis=1, keepdims=True) + 1e-06)
        unit = (x * inv).astype(BF16)
        full_ref[which * half : (which + 1) * half] = unit
        units.append(unit)

    @pl.when(core == 0)
    def _():
        near_ref[...] = units[1]
        far_ref[...] = units[0]

    @pl.when(core == 1)
    def _():
        near_ref[...] = units[0]
        far_ref[...] = units[1]


def near_kernel(core_ref, own_ref, sib_ref, n1_ref, n2_ref, sign_ref, e_ref, d_ref, sums_ref):
    core = core_ref[0]
    rows = own_ref.shape[0]
    chip = chip_rows(own_ref[...], sib_ref[...])
    near = chip_rows(n2_ref[...], n1_ref[...])
    for b in range(2):
        e = jnp.exp(gamma * rows_by_rows(chip[b * rows : (b + 1) * rows], near))
        e_ref[b * rows : (b + 1) * rows] = e

        @pl.when(core == 0)
        def _():
            sums_ref[b * rows : (b + 1) * rows, 2:3] = jnp.sum(e, axis=1, keepdims=True)

    @pl.when(core == 0)
    def _():
        for b in range(2):
            part = slice(b * rows, (b + 1) * rows)
            sign = sign_ref[part]
            d = jnp.exp(gamma * sign * rows_by_rows(chip[part], chip))
            d_ref[part] = d
            mine = sign[:, b * rows : (b + 1) * rows]
            here = d[:, b * rows : (b + 1) * rows]
            pos = jnp.where(mine < 0.0, here, 0.0)
            neg = jnp.where(mine > 0.0, here, 0.0)
            total = jnp.sum(neg, axis=1, keepdims=True)
            if b == 1:
                total = total + jnp.sum(d[:, 0:rows], axis=1, keepdims=True)
            sums_ref[part, 0:1] = jnp.sum(pos, axis=1, keepdims=True)
            sums_ref[part, 1:2] = total


def far_kernel(
    core_ref, own_ref, sib_ref, q1_ref, q2_ref, sums_ref, oa_ref, ob_ref,
    f_ref, cols_ref, lanes_ref, loss_ref,
):
    core = core_ref[0]
    rows = own_ref.shape[0]
    half = rows // 2
    far = jnp.concatenate([q2_ref[...], q1_ref[...]], axis=0)

    @pl.when(core == 1)
    def _():
        block = jnp.concatenate([own_ref[half:], sib_ref[half:]], axis=0)
        f_ref[...] = jnp.exp(gamma * rows_by_rows(block, far))

    @pl.when(core == 0)
    def _():
        block = jnp.concatenate([own_ref[0:half], sib_ref[0:half]], axis=0)
        f = jnp.exp(gamma * rows_by_rows(block, far))
        f_ref[...] = f
        ids = block_ids(rows, core, (rows, rows), 0)
        for b, order in enumerate((oa_ref, ob_ref)):
            part = slice(b * rows, (b + 1) * rows)
            pos_sum = sums_ref[part, 0:1]
            neg_sum = sums_ref[part, 1:2] + sums_ref[part, 2:3]
            if b == 0:
                neg_sum = neg_sum + jnp.sum(f, axis=1, keepdims=True)
            product = pos_sum * neg_sum
            weight = product / (1.0 + product)
            on_neg = gamma * weight / neg_sum
            on_pos = gamma * weight / pos_sum
            cols_ref[part, 0:1] = on_neg
            cols_ref[part, 1:2] = on_pos
            lanes_ref[0:1, part] = as_row(on_neg)
            lanes_ref[1:2, part] = as_row(on_pos)
            loss = jnp.log(1.0 + product)
            loss_ref[b : b + 1] = jnp.sum(
                jnp.where(ids == order[...], loss, 0.0), axis=0, keepdims=True
            )


def split_store(b, total, keep_ref, send_ref):
    half = total.shape[0] // 2
    keep_ref[b * half : (b + 1) * half] = total[0:half]
    send_ref[b * half : (b + 1) * half] = total[half:].astype(BF16)


def below_kernel(
    core_ref, own_ref, sib_ref, n1_ref, n2_ref, q1_ref, q2_ref,
    e_ref, d_ref, sign_ref, f_ref, cols_ref, lanes_ref, keep_ref, send_ref,
):
    core = core_ref[0]

    @pl.when(core == 0)
    def _():
        rows = own_ref.shape[0]
        chip = chip_rows(own_ref[...], sib_ref[...])
        near = chip_rows(n2_ref[...], n1_ref[...])
        far = jnp.concatenate([q2_ref[...], q1_ref[...]], axis=0)
        zero = jnp.zeros((1, rows), F32)
        for b in range(2):
            part = slice(b * rows, (b + 1) * rows)
            on_neg = cols_ref[part, 0:1]
            on_pos = cols_ref[part, 1:2]
            lanes_neg = lanes_ref[0:1]
            lanes_pos = lanes_ref[1:2]
            d = d_ref[part]
            sign = sign_ref[part]
            columns = []
            for other in range(2):
                there = slice(other * rows, (other + 1) * rows)
                if other == b:
                    here = sign[:, there]
                    up = on_neg + lanes_neg[:, there]
                    down = on_pos + lanes_pos[:, there]
                    scale = jnp.where(here > 0.0, up, jnp.where(here < 0.0, -down, 0.0))
                elif b == 0:
                    scale = lanes_neg[:, there]
                else:
                    scale = on_neg
                columns.append((scale * d[:, there]).astype(BF16))
            total = jnp.dot(jnp.concatenate(columns, axis=1), chip, preferred_element_type=F32)
            total = total + jnp.dot(
                (on_neg * e_ref[part]).astype(BF16), near, preferred_element_type=F32
            )
            if b == 0:
                total = total + jnp.dot(
                    (on_neg * f_ref[...]).astype(BF16), far, preferred_element_type=F32
                )
            split_store(b, total, keep_ref, send_ref)


def above_kernel(
    core_ref, n1_ref, n2_ref, q1_ref, q2_ref, e_ref, f_ref, near_ref, far_ref, keep_in, send_in,
    keep_ref, send_ref,
):
    core = core_ref[0]

    @pl.when(core == 1)
    def _():
        rows = n1_ref.shape[0]
        near = chip_rows(n2_ref[...], n1_ref[...])
        far = jnp.concatenate([q2_ref[...], q1_ref[...]], axis=0)
        for b in range(2):
            part = slice(b * rows, (b + 1) * rows)
            total = jnp.dot(
                (near_ref[...] * e_ref[part]).astype(BF16), near, preferred_element_type=F32
            )
            if b == 1:
                total = total + jnp.dot(
                    (far_ref[...] * f_ref[...]).astype(BF16), far, preferred_element_type=F32
                )
            split_store(b, total, keep_ref, send_ref)


def final_kernel(x_ref, keep_ref, other_ref, grad_ref):
    features = x_ref.shape[-1]
    half = keep_ref.shape[0] // 2
    for which in range(2):
        part = slice(which * half, (which + 1) * half)
        total = keep_ref[part] + other_ref[part].astype(F32)
        x = x_ref[:, which].astype(F32).reshape(half, features)
        inv = lax.rsqrt(jnp.sum(x * x, axis=1, keepdims=True) + 1e-06)
        u = x * inv
        grad = (total - u * jnp.sum(u * total, axis=1, keepdims=True)) * inv
        grad_ref[:, which] = grad.reshape(half // 8, 8, features).astype(BF16)


VMEM = pl.BlockSpec(memory_space=pltpu.VMEM)
SMEM = pl.BlockSpec(memory_space=pltpu.SMEM)


def shape(*size, dtype=F32):
    return jax.ShapeDtypeStruct(size, dtype)


def call(kernel, name, inputs, outputs, work, aliases=None):
    return pl.pallas_call(
        kernel,
        out_shape=outputs,
        in_specs=[SMEM if a.ndim == 1 else VMEM for a in inputs],
        out_specs=jax.tree.map(lambda _: VMEM, outputs),
        name=name,
        input_output_aliases=aliases or {},
        compiler_params=pltpu.CompilerParams(vmem_limit_bytes=LIMIT),
        cost_estimate=pl.CostEstimate(
            flops=int(work * 10**9), bytes_accessed=10**5, transcendentals=0
        ),
    )(*inputs)


def on_device(embeddings, order):
    rows, features = embeddings.shape
    peers = lax.axis_size(WHERE)
    per_peer = rows // peers
    half = rows // 2
    core = lax.axis_index("c").astype(jnp.int32).reshape(1)
    ring = lax.axis_size("y")

    def fetch_order(h):
        return lax.ppermute(order, ("c", "zh"), [(c * 2 + h, c) for c in range(2)])

    def send_loss(loss, h):
        return lax.ppermute(loss, ("c", "zh"), [(z, z * 2 + h) for z in range(2)])

    def along(value, moves):
        return lax.ppermute(
            value,
            ("c", "y"),
            [(a * ring + y, b * ring + (y + s) % ring) for a, b, s in moves for y in range(ring)],
        )

    oa, ob = fetch_order(0), fetch_order(1)
    arrived = lax.all_to_all(
        embeddings.reshape(peers, per_peer, features), WHERE, 0, 0, tiled=True
    ).reshape(peers // 2, 2, per_peer, features)
    sign = call(mask_kernel, "classes", (core, oa, ob), shape(2 * rows, 2 * rows), 0.5)

    own, near_half, far_half = call(
        pack_kernel,
        "pack",
        (core, arrived),
        (
            shape(rows, features, dtype=BF16),
            shape(half, features, dtype=BF16),
            shape(half, features, dtype=BF16),
        ),
        0.01,
    )
    n1 = along(own, ((0, 0, 1), (1, 1, -1)))
    n2 = along(own, ((1, 0, 1), (0, 1, -1)))
    sib = along(own, ((0, 1, 0), (1, 0, 0)))
    q1 = along(near_half, ((0, 0, 2), (1, 1, -2)))
    q2 = along(far_half, ((1, 0, 2), (0, 1, -2)))

    e, d, sums = call(
        near_kernel,
        "near",
        (core, own, sib, n1, n2, sign),
        (shape(2 * rows, 2 * rows), shape(2 * rows, 2 * rows), shape(2 * rows, 8)),
        1.2,
    )
    f, cols, lanes, loss = call(
        far_kernel,
        "far",
        (core, own, sib, q1, q2, sums, oa, ob),
        (shape(rows, rows), shape(2 * rows, 8), shape(2, 2 * rows), shape(2, rows)),
        0.2,
    )
    near_factor = along(lanes[0:1], ((0, 1, -1),))
    far_factor = along(lanes[0:1, 0:rows], ((0, 1, -2),))
    keep, send = call(
        below_kernel,
        "below",
        (core, own, sib, n1, n2, q1, q2, e, d, sign, f, cols, lanes),
        (shape(rows, features), shape(rows, features, dtype=BF16)),
        1.4,
    )
    keep, send = call(
        above_kernel,
        "above",
        (core, n1, n2, q1, q2, e, f, near_factor, far_factor, keep, send),
        (shape(rows, features), shape(rows, features, dtype=BF16)),
        0.8,
        {9: 0, 10: 1},
    )
    other = along(send, ((0, 1, 0), (1, 0, 0)))
    grad = call(
        final_kernel,
        "final",
        (arrived, keep, other),
        shape(peers // 2, 2, per_peer, features, dtype=BF16),
        0.01,
    )
    row_loss = send_loss(loss[0:1], 0) + send_loss(loss[1:2], 1)
    sent_back = lax.all_to_all(
        grad.reshape(peers, per_peer, features), WHERE, 0, 0, tiled=True
    )
    return sent_back.reshape(rows, features), row_loss


def solution(mesh):
    dp, grp = mesh.devices.shape
    parts = Mesh(
        mesh.devices.reshape(dp // 8, 4, 2, grp // 2, 2), ("zl", "x", "c", "y", "zh")
    )
    placed = P(("zl", "x", "c", "y", "zh"), None)
    return jax.shard_map(
        on_device, mesh=parts, in_specs=(placed, placed), out_specs=(placed, placed), check_vma=False
    )
```

```python
import jax
import jax.numpy as jnp
from jax import lax
from jax.experimental import pallas as pl
from jax.experimental.pallas import tpu as pltpu
from jax.sharding import Mesh
from jax.sharding import PartitionSpec as P


K = 16
gamma = 16.0
F32 = jnp.float32
BF16 = jnp.bfloat16
WHERE = ("zl", "x", "zh")
LIMIT = 20 * 2**20


def rows_by_rows(a, b):
    return lax.dot_general(a, b, (((1,), (1,)), ((), ())), preferred_element_type=F32)


def block_ids(rows, core, shape, axis):
    half = rows // 2
    i = lax.broadcasted_iota(jnp.int32, shape, axis)
    source = jnp.where(i < half, core, 1 - core)
    i = jnp.where(i < half, i, i - half)
    return (i // 8) * 16 + source * 8 + i % 8


def chip_rows(own, sib):
    half = own.shape[0] // 2
    return jnp.concatenate([own[0:half], sib[0:half], own[half:], sib[half:]], axis=0)


def as_row(column):
    return jnp.broadcast_to(column, (column.shape[0], 128)).T[0:1]


def mask_kernel(core_ref, oa_ref, ob_ref, sign_ref):
    core = core_ref[0]

    @pl.when(core == 0)
    def _():
        rows = oa_ref.shape[1]
        ids = block_ids(rows, core, (rows, rows), 0)
        slot = lax.broadcasted_iota(jnp.int32, (rows, 128), 0) // K
        kind = lax.broadcasted_iota(jnp.int32, (rows, 128), 1)
        hot = []
        for which, ref in enumerate((oa_ref, ob_ref)):
            chosen = jnp.where(ids == ref[...], 1.0, 0.0).astype(BF16)
            table = jnp.where(kind == slot + which * (rows // K), 1.0, 0.0).astype(BF16)
            hot.append(jnp.dot(chosen, table, preferred_element_type=F32).astype(BF16))
        hot = jnp.concatenate(hot, axis=0)
        same = rows_by_rows(hot, hot)
        shape = (2 * rows, 2 * rows)
        diagonal = lax.broadcasted_iota(jnp.int32, shape, 0) == lax.broadcasted_iota(
            jnp.int32, shape, 1
        )
        sign_ref[...] = jnp.where(diagonal, 0.0, 1.0 - 2.0 * same)


def pack_kernel(x_ref, oa_ref, ob_ref, full_ref):
    half = full_ref.shape[0] // 2
    for which in range(2):
        x = x_ref[:, which].astype(F32).reshape(half, x_ref.shape[-1])
        inv = lax.rsqrt(jnp.sum(x * x, axis=1, keepdims=True) + 1e-06)
        full_ref[which * half : (which + 1) * half] = (x * inv).astype(BF16)


def relay_kernel(core_ref, n1_ref, n2_ref, out_ref):
    half = n1_ref.shape[0] // 2
    for c in range(2):

        @pl.when(core_ref[0] == c)
        def _():
            part = slice((1 - c) * half, (2 - c) * half)
            out_ref[0:half] = n2_ref[part]
            out_ref[half:] = n1_ref[part]


def near_kernel(core_ref, own_ref, sib_ref, n1_ref, n2_ref, e_ref, sums_ref):
    core = core_ref[0]
    rows = own_ref.shape[0]
    chip = chip_rows(own_ref[...], sib_ref[...])
    near = chip_rows(n2_ref[...], n1_ref[...])
    for b in range(2):
        e = jnp.exp(gamma * rows_by_rows(chip[b * rows : (b + 1) * rows], near))
        e_ref[b * rows : (b + 1) * rows] = e

        @pl.when(core == 0)
        def _():
            sums_ref[b * rows : (b + 1) * rows, 0:1] = jnp.sum(e, axis=1, keepdims=True)


def own_kernel(core_ref, own_ref, sib_ref, sign_ref, d_ref, sums_ref):
    @pl.when(core_ref[0] == 0)
    def _():
        rows = own_ref.shape[0]
        chip = chip_rows(own_ref[...], sib_ref[...])
        for b in range(2):
            part = slice(b * rows, (b + 1) * rows)
            sign = sign_ref[part]
            d = jnp.exp(gamma * sign * rows_by_rows(chip[part], chip))
            d_ref[part] = d
            mine = sign[:, b * rows : (b + 1) * rows]
            here = d[:, b * rows : (b + 1) * rows]
            pos = jnp.where(mine < 0.0, here, 0.0)
            neg = jnp.where(mine > 0.0, here, 0.0)
            total = jnp.sum(neg, axis=1, keepdims=True)
            if b == 1:
                total = total + jnp.sum(d[:, 0:rows], axis=1, keepdims=True)
            sums_ref[part, 0:1] = jnp.sum(pos, axis=1, keepdims=True)
            sums_ref[part, 1:2] = total


def far_kernel(
    core_ref, own_ref, sib_ref, far_ref, near_sums_ref, sums_ref, oa_ref, ob_ref,
    f_ref, cols_ref, lanes_ref, loss_ref,
):
    core = core_ref[0]
    rows = own_ref.shape[0]
    half = rows // 2
    far = far_ref[...]

    @pl.when(core == 1)
    def _():
        block = jnp.concatenate([own_ref[half:], sib_ref[half:]], axis=0)
        f_ref[...] = jnp.exp(gamma * rows_by_rows(block, far))

    @pl.when(core == 0)
    def _():
        block = jnp.concatenate([own_ref[0:half], sib_ref[0:half]], axis=0)
        f = jnp.exp(gamma * rows_by_rows(block, far))
        f_ref[...] = f
        ids = block_ids(rows, core, (rows, rows), 0)
        for b, order in enumerate((oa_ref, ob_ref)):
            part = slice(b * rows, (b + 1) * rows)
            pos_sum = sums_ref[part, 0:1]
            neg_sum = sums_ref[part, 1:2] + near_sums_ref[part, 0:1]
            if b == 0:
                neg_sum = neg_sum + jnp.sum(f, axis=1, keepdims=True)
            product = pos_sum * neg_sum
            weight = product / (1.0 + product)
            on_neg = gamma * weight / neg_sum
            on_pos = gamma * weight / pos_sum
            cols_ref[part, 0:1] = on_neg
            cols_ref[part, 1:2] = on_pos
            lanes_ref[0:1, part] = as_row(on_neg)
            lanes_ref[1:2, part] = as_row(on_pos)
            loss = jnp.log(1.0 + product)
            loss_ref[b : b + 1] = jnp.sum(
                jnp.where(ids == order[...], loss, 0.0), axis=0, keepdims=True
            )


def split_store(b, total, keep_ref, send_ref):
    half = total.shape[0] // 2
    keep_ref[b * half : (b + 1) * half] = total[0:half]
    send_ref[b * half : (b + 1) * half] = total[half:]


def below_kernel(
    core_ref, own_ref, sib_ref, n1_ref, n2_ref, far_ref,
    e_ref, d_ref, sign_ref, f_ref, cols_ref, lanes_ref, keep_ref, send_ref,
):
    core = core_ref[0]

    @pl.when(core == 0)
    def _():
        rows = own_ref.shape[0]
        chip = chip_rows(own_ref[...], sib_ref[...])
        near = chip_rows(n2_ref[...], n1_ref[...])
        far = far_ref[...]
        zero = jnp.zeros((1, rows), F32)
        for b in range(2):
            part = slice(b * rows, (b + 1) * rows)
            on_neg = cols_ref[part, 0:1]
            on_pos = cols_ref[part, 1:2]
            lanes_neg = lanes_ref[0:1]
            lanes_pos = lanes_ref[1:2]
            d = d_ref[part]
            sign = sign_ref[part]
            columns = []
            for other in range(2):
                there = slice(other * rows, (other + 1) * rows)
                if other == b:
                    here = sign[:, there]
                    up = on_neg + lanes_neg[:, there]
                    down = on_pos + lanes_pos[:, there]
                    scale = jnp.where(here > 0.0, up, jnp.where(here < 0.0, -down, 0.0))
                elif b == 0:
                    scale = lanes_neg[:, there]
                else:
                    scale = on_neg
                columns.append((scale * d[:, there]).astype(BF16))
            total = jnp.dot(jnp.concatenate(columns, axis=1), chip, preferred_element_type=F32)
            total = total + jnp.dot(
                (on_neg * e_ref[part]).astype(BF16), near, preferred_element_type=F32
            )
            if b == 0:
                total = total + jnp.dot(
                    (on_neg * f_ref[...]).astype(BF16), far, preferred_element_type=F32
                )
            split_store(b, total, keep_ref, send_ref)


def above_kernel(
    core_ref, n1_ref, n2_ref, far_ref, e_ref, f_ref, on_near_ref, on_far_ref, keep_in, send_in,
    keep_ref, send_ref,
):
    core = core_ref[0]

    @pl.when(core == 1)
    def _():
        rows = n1_ref.shape[0]
        near = chip_rows(n2_ref[...], n1_ref[...])
        far = far_ref[...]
        for b in range(2):
            part = slice(b * rows, (b + 1) * rows)
            total = jnp.dot(
                (on_near_ref[...] * e_ref[part]).astype(BF16), near, preferred_element_type=F32
            )
            if b == 1:
                total = total + jnp.dot(
                    (on_far_ref[...] * f_ref[...]).astype(BF16), far, preferred_element_type=F32
                )
            split_store(b, total, keep_ref, send_ref)


def final_kernel(x_ref, keep_ref, other_ref, la_ref, lb_ref, grad_ref, loss_ref):
    loss_ref[...] = la_ref[...] + lb_ref[...]
    features = x_ref.shape[-1]
    half = keep_ref.shape[0] // 2
    for which in range(2):
        part = slice(which * half, (which + 1) * half)
        total = keep_ref[part] + other_ref[part]
        x = x_ref[:, which].astype(F32).reshape(half, features)
        inv = lax.rsqrt(jnp.sum(x * x, axis=1, keepdims=True) + 1e-06)
        u = x * inv
        grad = (total - u * jnp.sum(u * total, axis=1, keepdims=True)) * inv
        grad_ref[:, which] = grad.reshape(half // 8, 8, features).astype(BF16)


VMEM = pl.BlockSpec(memory_space=pltpu.VMEM)
SMEM = pl.BlockSpec(memory_space=pltpu.SMEM)


def shape(*size, dtype=F32):
    return jax.ShapeDtypeStruct(size, dtype)


def call(kernel, name, inputs, outputs, work, aliases=None):
    return pl.pallas_call(
        kernel,
        out_shape=outputs,
        in_specs=[SMEM if a.ndim == 1 else VMEM for a in inputs],
        out_specs=jax.tree.map(lambda _: VMEM, outputs),
        name=name,
        input_output_aliases=aliases or {},
        compiler_params=pltpu.CompilerParams(vmem_limit_bytes=LIMIT),
        cost_estimate=pl.CostEstimate(
            flops=int(work * 10**9), bytes_accessed=10**5, transcendentals=0
        ),
    )(*inputs)


def on_device(embeddings, order):
    rows, features = embeddings.shape
    peers = lax.axis_size(WHERE)
    per_peer = rows // peers
    half = rows // 2
    core = lax.axis_index("c").astype(jnp.int32).reshape(1)
    ring = lax.axis_size("y")

    def fetch_order(h):
        return lax.ppermute(order, ("c", "zh"), [(c * 2 + h, c) for c in range(2)])

    def send_loss(loss, h):
        return lax.ppermute(loss, ("c", "zh"), [(z, z * 2 + h) for z in range(2)])

    def along(value, moves):
        return lax.ppermute(
            value,
            ("c", "y"),
            [(a * ring + y, b * ring + (y + s) % ring) for a, b, s in moves for y in range(ring)],
        )

    oa, ob = fetch_order(0), fetch_order(1)
    arrived = lax.all_to_all(
        embeddings.reshape(peers, per_peer, features), WHERE, 0, 0, tiled=True
    ).reshape(peers // 2, 2, per_peer, features)
    block = shape(rows, features, dtype=BF16)

    own = call(pack_kernel, "pack", (arrived, oa, ob), block, 0.01)
    n1 = along(own, ((0, 0, 1), (1, 1, -1)))
    n2 = along(own, ((1, 0, 1), (0, 1, -1)))
    sib = along(own, ((0, 1, 0), (1, 0, 0)))
    relay = call(relay_kernel, "relay", (core, n1, n2), block, 0.01)
    far = along(relay, ((0, 0, 1), (1, 1, -1)))

    sign = call(mask_kernel, "classes", (core, oa, ob), shape(2 * rows, 2 * rows), 0.5)
    e, near_sums = call(
        near_kernel,
        "near",
        (core, own, sib, n1, n2),
        (shape(2 * rows, 2 * rows), shape(2 * rows, 8)),
        0.8,
    )
    d, own_sums = call(
        own_kernel,
        "own",
        (core, own, sib, sign),
        (shape(2 * rows, 2 * rows), shape(2 * rows, 8)),
        0.8,
    )
    f, cols, lanes, loss = call(
        far_kernel,
        "far",
        (core, own, sib, far, near_sums, own_sums, oa, ob),
        (shape(rows, rows), shape(2 * rows, 8), shape(2, 2 * rows), shape(2, rows)),
        0.2,
    )
    on_near = along(lanes[0:1], ((0, 1, -1),))
    on_far = along(lanes[0:1, 0:rows], ((0, 1, -2),))
    half_grads = (shape(rows, features), shape(rows, features))
    keep, send = call(
        below_kernel,
        "below",
        (core, own, sib, n1, n2, far, e, d, sign, f, cols, lanes),
        half_grads,
        1.4,
    )
    keep, send = call(
        above_kernel,
        "above",
        (core, n1, n2, far, e, f, on_near, on_far, keep, send),
        half_grads,
        0.8,
        {8: 0, 9: 1},
    )
    other = along(send, ((0, 1, 0), (1, 0, 0)))
    grad, row_loss = call(
        final_kernel,
        "final",
        (arrived, keep, other, send_loss(loss[0:1], 0), send_loss(loss[1:2], 1)),
        (shape(peers // 2, 2, per_peer, features, dtype=BF16), shape(1, rows)),
        0.01,
    )
    sent_back = lax.all_to_all(
        grad.reshape(peers, per_peer, features), WHERE, 0, 0, tiled=True
    )
    return sent_back.reshape(rows, features), row_loss


def solution(mesh):
    dp, grp = mesh.devices.shape
    parts = Mesh(
        mesh.devices.reshape(dp // 8, 4, 2, grp // 2, 2), ("zl", "x", "c", "y", "zh")
    )
    placed = P(("zl", "x", "c", "y", "zh"), None)
    return jax.shard_map(
        on_device, mesh=parts, in_specs=(placed, placed), out_specs=(placed, placed), check_vma=False
    )
```

```python
import jax
import jax.numpy as jnp
from jax import lax
from jax.experimental import pallas as pl
from jax.experimental.pallas import tpu as pltpu
from jax.sharding import Mesh
from jax.sharding import PartitionSpec as P


K = 16
gamma = 16.0
F32 = jnp.float32
BF16 = jnp.bfloat16
WHERE = ("zl", "x", "zh")
LIMIT = 20 * 2**20


def rows_by_rows(a, b):
    return lax.dot_general(a, b, (((1,), (1,)), ((), ())), preferred_element_type=F32)


def block_ids(rows, core, shape, axis):
    half = rows // 2
    i = lax.broadcasted_iota(jnp.int32, shape, axis)
    source = jnp.where(i < half, core, 1 - core)
    i = jnp.where(i < half, i, i - half)
    return (i // 8) * 16 + source * 8 + i % 8


def chip_rows(own, sib):
    half = own.shape[0] // 2
    return jnp.concatenate([own[0:half], sib[0:half], own[half:], sib[half:]], axis=0)


def as_row(column):
    return jnp.broadcast_to(column, (column.shape[0], 128)).T[0:1]


def mask_kernel(core_ref, oa_ref, ob_ref, sign_ref):
    core = core_ref[0]

    @pl.when(core == 0)
    def _():
        rows = oa_ref.shape[1]
        ids = block_ids(rows, core, (rows, rows), 0)
        slot = lax.broadcasted_iota(jnp.int32, (rows, 128), 0) // K
        kind = lax.broadcasted_iota(jnp.int32, (rows, 128), 1)
        hot = []
        for which, ref in enumerate((oa_ref, ob_ref)):
            chosen = jnp.where(ids == ref[...], 1.0, 0.0).astype(BF16)
            table = jnp.where(kind == slot + which * (rows // K), 1.0, 0.0).astype(BF16)
            hot.append(jnp.dot(chosen, table, preferred_element_type=F32).astype(BF16))
        hot = jnp.concatenate(hot, axis=0)
        same = rows_by_rows(hot, hot)
        shape = (2 * rows, 2 * rows)
        diagonal = lax.broadcasted_iota(jnp.int32, shape, 0) == lax.broadcasted_iota(
            jnp.int32, shape, 1
        )
        sign_ref[...] = jnp.where(diagonal, 0.0, 1.0 - 2.0 * same)


def pack_kernel(core_ref, x_ref, oa_ref, ob_ref, full_ref, one_ref, two_ref):
    core = core_ref[0]
    half = one_ref.shape[0]
    for which in range(2):
        x = x_ref[:, which].astype(F32).reshape(half, x_ref.shape[-1])
        inv = lax.rsqrt(jnp.sum(x * x, axis=1, keepdims=True) + 1e-06)
        unit = (x * inv).astype(BF16)
        full_ref[which * half : (which + 1) * half] = unit

        @pl.when(core == 1 - which)
        def _():
            one_ref[...] = unit

        @pl.when(core == which)
        def _():
            two_ref[...] = unit


def near_kernel(core_ref, own_ref, sib_ref, n1_ref, n2_ref, e_ref, sums_ref):
    core = core_ref[0]
    rows = own_ref.shape[0]
    chip = chip_rows(own_ref[...], sib_ref[...])
    near = chip_rows(n2_ref[...], n1_ref[...])
    for b in range(2):
        e = jnp.exp(gamma * rows_by_rows(chip[b * rows : (b + 1) * rows], near))
        e_ref[b * rows : (b + 1) * rows] = e

        @pl.when(core == 0)
        def _():
            sums_ref[b * rows : (b + 1) * rows, 0:1] = jnp.sum(e, axis=1, keepdims=True)


def own_kernel(core_ref, own_ref, sib_ref, sign_ref, d_ref, sums_ref):
    @pl.when(core_ref[0] == 0)
    def _():
        rows = own_ref.shape[0]
        chip = chip_rows(own_ref[...], sib_ref[...])
        for b in range(2):
            part = slice(b * rows, (b + 1) * rows)
            sign = sign_ref[part]
            d = jnp.exp(gamma * sign * rows_by_rows(chip[part], chip))
            d_ref[part] = d
            mine = sign[:, b * rows : (b + 1) * rows]
            here = d[:, b * rows : (b + 1) * rows]
            pos = jnp.where(mine < 0.0, here, 0.0)
            neg = jnp.where(mine > 0.0, here, 0.0)
            total = jnp.sum(neg, axis=1, keepdims=True)
            if b == 1:
                total = total + jnp.sum(d[:, 0:rows], axis=1, keepdims=True)
            sums_ref[part, 0:1] = jnp.sum(pos, axis=1, keepdims=True)
            sums_ref[part, 1:2] = total


def far_kernel(
    core_ref, own_ref, sib_ref, q1_ref, q2_ref, near_sums_ref, sums_ref, oa_ref, ob_ref,
    f_ref, cols_ref, lanes_ref, loss_ref,
):
    core = core_ref[0]
    rows = own_ref.shape[0]
    half = rows // 2
    far = jnp.concatenate([q2_ref[...], q1_ref[...]], axis=0)

    @pl.when(core == 1)
    def _():
        block = jnp.concatenate([own_ref[half:], sib_ref[half:]], axis=0)
        f_ref[...] = jnp.exp(gamma * rows_by_rows(block, far))

    @pl.when(core == 0)
    def _():
        block = jnp.concatenate([own_ref[0:half], sib_ref[0:half]], axis=0)
        f = jnp.exp(gamma * rows_by_rows(block, far))
        f_ref[...] = f
        ids = block_ids(rows, core, (rows, rows), 0)
        for b, order in enumerate((oa_ref, ob_ref)):
            part = slice(b * rows, (b + 1) * rows)
            pos_sum = sums_ref[part, 0:1]
            neg_sum = sums_ref[part, 1:2] + near_sums_ref[part, 0:1]
            if b == 0:
                neg_sum = neg_sum + jnp.sum(f, axis=1, keepdims=True)
            product = pos_sum * neg_sum
            weight = product / (1.0 + product)
            on_neg = gamma * weight / neg_sum
            on_pos = gamma * weight / pos_sum
            cols_ref[part, 0:1] = on_neg
            cols_ref[part, 1:2] = on_pos
            lanes_ref[0:1, part] = as_row(on_neg)
            lanes_ref[1:2, part] = as_row(on_pos)
            loss = jnp.log(1.0 + product)
            loss_ref[b : b + 1] = jnp.sum(
                jnp.where(ids == order[...], loss, 0.0), axis=0, keepdims=True
            )


def split_store(b, total, keep_ref, send_ref):
    half = total.shape[0] // 2
    keep_ref[b * half : (b + 1) * half] = total[0:half]
    send_ref[b * half : (b + 1) * half] = total[half:]


def below_kernel(
    core_ref, own_ref, sib_ref, n1_ref, n2_ref, q1_ref, q2_ref,
    e_ref, d_ref, sign_ref, f_ref, cols_ref, lanes_ref, keep_ref, send_ref,
):
    core = core_ref[0]

    @pl.when(core == 0)
    def _():
        rows = own_ref.shape[0]
        chip = chip_rows(own_ref[...], sib_ref[...])
        near = chip_rows(n2_ref[...], n1_ref[...])
        far = jnp.concatenate([q2_ref[...], q1_ref[...]], axis=0)
        zero = jnp.zeros((1, rows), F32)
        for b in range(2):
            part = slice(b * rows, (b + 1) * rows)
            on_neg = cols_ref[part, 0:1]
            on_pos = cols_ref[part, 1:2]
            lanes_neg = lanes_ref[0:1]
            lanes_pos = lanes_ref[1:2]
            d = d_ref[part]
            sign = sign_ref[part]
            columns = []
            for other in range(2):
                there = slice(other * rows, (other + 1) * rows)
                if other == b:
                    here = sign[:, there]
                    up = on_neg + lanes_neg[:, there]
                    down = on_pos + lanes_pos[:, there]
                    scale = jnp.where(here > 0.0, up, jnp.where(here < 0.0, -down, 0.0))
                elif b == 0:
                    scale = lanes_neg[:, there]
                else:
                    scale = on_neg
                columns.append((scale * d[:, there]).astype(BF16))
            total = jnp.dot(jnp.concatenate(columns, axis=1), chip, preferred_element_type=F32)
            total = total + jnp.dot(
                (on_neg * e_ref[part]).astype(BF16), near, preferred_element_type=F32
            )
            if b == 0:
                total = total + jnp.dot(
                    (on_neg * f_ref[...]).astype(BF16), far, preferred_element_type=F32
                )
            split_store(b, total, keep_ref, send_ref)


def above_kernel(
    core_ref, n1_ref, n2_ref, q1_ref, q2_ref, e_ref, f_ref, on_near_ref, on_far_ref, keep_in, send_in,
    keep_ref, send_ref,
):
    core = core_ref[0]

    @pl.when(core == 1)
    def _():
        rows = n1_ref.shape[0]
        near = chip_rows(n2_ref[...], n1_ref[...])
        far = jnp.concatenate([q2_ref[...], q1_ref[...]], axis=0)
        for b in range(2):
            part = slice(b * rows, (b + 1) * rows)
            total = jnp.dot(
                (on_near_ref[...] * e_ref[part]).astype(BF16), near, preferred_element_type=F32
            )
            if b == 1:
                total = total + jnp.dot(
                    (on_far_ref[...] * f_ref[...]).astype(BF16), far, preferred_element_type=F32
                )
            split_store(b, total, keep_ref, send_ref)


def final_kernel(x_ref, keep_ref, other_ref, la_ref, lb_ref, grad_ref, loss_ref):
    loss_ref[...] = la_ref[...] + lb_ref[...]
    features = x_ref.shape[-1]
    half = keep_ref.shape[0] // 2
    for which in range(2):
        part = slice(which * half, (which + 1) * half)
        total = keep_ref[part] + other_ref[part]
        x = x_ref[:, which].astype(F32).reshape(half, features)
        inv = lax.rsqrt(jnp.sum(x * x, axis=1, keepdims=True) + 1e-06)
        u = x * inv
        grad = (total - u * jnp.sum(u * total, axis=1, keepdims=True)) * inv
        grad_ref[:, which] = grad.reshape(half // 8, 8, features).astype(BF16)


VMEM = pl.BlockSpec(memory_space=pltpu.VMEM)
SMEM = pl.BlockSpec(memory_space=pltpu.SMEM)


def shape(*size, dtype=F32):
    return jax.ShapeDtypeStruct(size, dtype)


def call(kernel, inputs, outputs, work, aliases=None):
    return pl.pallas_call(
        kernel,
        out_shape=outputs,
        in_specs=[SMEM if a.ndim == 1 else VMEM for a in inputs],
        out_specs=jax.tree.map(lambda _: VMEM, outputs),
        input_output_aliases=aliases or {},
        compiler_params=pltpu.CompilerParams(vmem_limit_bytes=LIMIT),
        cost_estimate=pl.CostEstimate(
            flops=int(work * 10**9), bytes_accessed=10**5, transcendentals=0
        ),
    )(*inputs)


def on_device(embeddings, order):
    rows, features = embeddings.shape
    peers = lax.axis_size(WHERE)
    per_peer = rows // peers
    half = rows // 2
    core = lax.axis_index("c").astype(jnp.int32).reshape(1)
    ring = lax.axis_size("y")

    def fetch_order(h):
        return lax.ppermute(order, ("c", "zh"), [(c * 2 + h, c) for c in range(2)])

    def send_loss(loss, h):
        return lax.ppermute(loss, ("c", "zh"), [(z, z * 2 + h) for z in range(2)])

    def along(value, moves):
        route = [(a * ring + y, b * ring + (y + s) % ring) for a, b, s in moves for y in range(ring)]
        return lax.ppermute(value, ("c", "y"), route)

    oa, ob = fetch_order(0), fetch_order(1)
    arrived = lax.all_to_all(
        embeddings.reshape(peers, per_peer, features), WHERE, 0, 0, tiled=True
    ).reshape(peers // 2, 2, per_peer, features)
    block = shape(rows, features, dtype=BF16)
    half_block = shape(half, features, dtype=BF16)

    own, one, two = call(
        pack_kernel, (core, arrived, oa, ob), (block, half_block, half_block), 0.01
    )
    n1 = along(own, ((0, 0, 1), (1, 1, -1)))
    n2 = along(own, ((1, 0, 1), (0, 1, -1)))
    q1 = along(one, ((0, 0, 2), (1, 1, -2)))
    q2 = along(two, ((1, 0, 2), (0, 1, -2)))
    sib = along(own, ((0, 1, 0), (1, 0, 0)))

    sign = call(mask_kernel, (core, oa, ob), shape(2 * rows, 2 * rows), 0.5)
    e, near_sums = call(
        near_kernel, (core, own, sib, n1, n2), (shape(2 * rows, 2 * rows), shape(2 * rows, 8)), 0.8
    )
    d, own_sums = call(
        own_kernel, (core, own, sib, sign), (shape(2 * rows, 2 * rows), shape(2 * rows, 8)), 0.8
    )
    f, cols, lanes, loss = call(
        far_kernel,
        (core, own, sib, q1, q2, near_sums, own_sums, oa, ob),
        (shape(rows, rows), shape(2 * rows, 8), shape(2, 2 * rows), shape(2, rows)),
        0.2,
    )
    on_near = along(lanes[0:1], ((0, 1, -1),))
    on_far = along(lanes[0:1, 0:rows], ((0, 1, -2),))
    half_grads = (shape(rows, features), shape(rows, features))
    keep, send = call(
        below_kernel, (core, own, sib, n1, n2, q1, q2, e, d, sign, f, cols, lanes), half_grads, 1.4
    )
    keep, send = call(
        above_kernel,
        (core, n1, n2, q1, q2, e, f, on_near, on_far, keep, send),
        half_grads,
        0.8,
        {9: 0, 10: 1},
    )
    other = along(send, ((0, 1, 0), (1, 0, 0)))
    grad, row_loss = call(
        final_kernel,
        (arrived, keep, other, send_loss(loss[0:1], 0), send_loss(loss[1:2], 1)),
        (shape(peers // 2, 2, per_peer, features, dtype=BF16), shape(1, rows)),
        0.01,
    )
    sent_back = lax.all_to_all(
        grad.reshape(peers, per_peer, features), WHERE, 0, 0, tiled=True
    )
    return sent_back.reshape(rows, features), row_loss


def solution(mesh):
    dp, grp = mesh.devices.shape
    parts = Mesh(
        mesh.devices.reshape(dp // 8, 4, 2, grp // 2, 2), ("zl", "x", "c", "y", "zh")
    )
    placed = P(("zl", "x", "c", "y", "zh"), None)

    def step(embeddings, order):
        return on_device(embeddings, order)

    step = jax.shard_map(
        step, mesh=parts, in_specs=(placed, placed), out_specs=(placed, placed), check_vma=False
    )
    return step
```

```python
import jax
import jax.numpy as jnp
from jax import lax
from jax.experimental import pallas as pl
from jax.experimental.pallas import tpu as pltpu
from jax.sharding import Mesh
from jax.sharding import PartitionSpec as P


K = 16
gamma = 16.0
F32 = jnp.float32
BF16 = jnp.bfloat16
WHERE = ("zl", "x", "zh")
LIMIT = 20 * 2**20


def rows_by_rows(a, b):
    return lax.dot_general(a, b, (((1,), (1,)), ((), ())), preferred_element_type=F32)


def block_ids(rows, core, shape, axis):
    half = rows // 2
    i = lax.broadcasted_iota(jnp.int32, shape, axis)
    source = jnp.where(i < half, core, 1 - core)
    i = jnp.where(i < half, i, i - half)
    return (i // 8) * 16 + source * 8 + i % 8


def chip_rows(own, sib):
    half = own.shape[0] // 2
    return jnp.concatenate([own[0:half], sib[0:half], own[half:], sib[half:]], axis=0)


def as_row(column):
    return jnp.broadcast_to(column, (column.shape[0], 128)).T[0:1]


def mask_kernel(core_ref, oa_ref, ob_ref, sign_ref):
    core = core_ref[0]

    @pl.when(core == 0)
    def _():
        rows = oa_ref.shape[1]
        ids = block_ids(rows, core, (rows, rows), 0)
        slot = lax.broadcasted_iota(jnp.int32, (rows, 128), 0) // K
        kind = lax.broadcasted_iota(jnp.int32, (rows, 128), 1)
        hot = []
        for which, ref in enumerate((oa_ref, ob_ref)):
            chosen = jnp.where(ids == ref[...], 1.0, 0.0).astype(BF16)
            table = jnp.where(kind == slot + which * (rows // K), 1.0, 0.0).astype(BF16)
            hot.append(jnp.dot(chosen, table, preferred_element_type=F32).astype(BF16))
        hot = jnp.concatenate(hot, axis=0)
        same = rows_by_rows(hot, hot)
        shape = (2 * rows, 2 * rows)
        diagonal = lax.broadcasted_iota(jnp.int32, shape, 0) == lax.broadcasted_iota(
            jnp.int32, shape, 1
        )
        sign_ref[...] = jnp.where(diagonal, 0.0, 1.0 - 2.0 * same)


def pack_kernel(core_ref, x_ref, oa_ref, ob_ref, full_ref, one_ref, two_ref):
    core = core_ref[0]
    half = one_ref.shape[0]
    for which in range(2):
        x = x_ref[:, which].astype(F32).reshape(half, x_ref.shape[-1])
        inv = lax.rsqrt(jnp.sum(x * x, axis=1, keepdims=True) + 1e-06)
        unit = (x * inv).astype(BF16)
        full_ref[which * half : (which + 1) * half] = unit

        @pl.when(core == 1 - which)
        def _():
            one_ref[...] = unit

        @pl.when(core == which)
        def _():
            two_ref[...] = unit


def relay_kernel(n1a_ref, n2a_ref, out_ref):
    half = n1a_ref.shape[0]
    out_ref[0:half] = n2a_ref[...]
    out_ref[half:] = n1a_ref[...]


def near_rows(n1a, n2a, n1b, n2b):
    return jnp.concatenate([n2b[...], n1b[...], n2a[...], n1a[...]], axis=0)


def near_kernel(
    core_ref, own_ref, sib_ref, n1a_ref, n2a_ref, n1b_ref, n2b_ref, e_ref, sums_ref
):
    core = core_ref[0]
    rows = own_ref.shape[0]
    chip = chip_rows(own_ref[...], sib_ref[...])
    near = near_rows(n1a_ref, n2a_ref, n1b_ref, n2b_ref)
    for b in range(2):
        e = jnp.exp(gamma * rows_by_rows(chip[b * rows : (b + 1) * rows], near))
        e_ref[b * rows : (b + 1) * rows] = e

        @pl.when(core == 0)
        def _():
            sums_ref[b * rows : (b + 1) * rows, 0:1] = jnp.sum(e, axis=1, keepdims=True)


def own_kernel(core_ref, own_ref, sib_ref, sign_ref, d_ref, sums_ref):
    @pl.when(core_ref[0] == 0)
    def _():
        rows = own_ref.shape[0]
        chip = chip_rows(own_ref[...], sib_ref[...])
        for b in range(2):
            part = slice(b * rows, (b + 1) * rows)
            sign = sign_ref[part]
            d = jnp.exp(gamma * sign * rows_by_rows(chip[part], chip))
            d_ref[part] = d
            mine = sign[:, b * rows : (b + 1) * rows]
            here = d[:, b * rows : (b + 1) * rows]
            pos = jnp.where(mine < 0.0, here, 0.0)
            neg = jnp.where(mine > 0.0, here, 0.0)
            total = jnp.sum(neg, axis=1, keepdims=True)
            if b == 1:
                total = total + jnp.sum(d[:, 0:rows], axis=1, keepdims=True)
            sums_ref[part, 0:1] = jnp.sum(pos, axis=1, keepdims=True)
            sums_ref[part, 1:2] = total


def far_kernel(
    core_ref, own_ref, sib_ref, far_ref, near_sums_ref, sums_ref, oa_ref, ob_ref,
    f_ref, cols_ref, lanes_ref, loss_ref, to_near_ref, to_far_ref,
):
    core = core_ref[0]
    rows = own_ref.shape[0]
    half = rows // 2
    far = far_ref[...]

    @pl.when(core == 1)
    def _():
        block = jnp.concatenate([own_ref[half:], sib_ref[half:]], axis=0)
        f_ref[...] = jnp.exp(gamma * rows_by_rows(block, far))

    @pl.when(core == 0)
    def _():
        block = jnp.concatenate([own_ref[0:half], sib_ref[0:half]], axis=0)
        f = jnp.exp(gamma * rows_by_rows(block, far))
        f_ref[...] = f
        ids = block_ids(rows, core, (rows, rows), 0)
        for b, order in enumerate((oa_ref, ob_ref)):
            part = slice(b * rows, (b + 1) * rows)
            pos_sum = sums_ref[part, 0:1]
            neg_sum = sums_ref[part, 1:2] + near_sums_ref[part, 0:1]
            if b == 0:
                neg_sum = neg_sum + jnp.sum(f, axis=1, keepdims=True)
            product = pos_sum * neg_sum
            weight = product / (1.0 + product)
            on_neg = gamma * weight / neg_sum
            on_pos = gamma * weight / pos_sum
            cols_ref[part, 0:1] = on_neg
            cols_ref[part, 1:2] = on_pos
            row = as_row(on_neg)
            lanes_ref[0:1, part] = row
            to_near_ref[0:1, (1 - b) * rows : (2 - b) * rows] = row
            if b == 0:
                to_far_ref[...] = row
            lanes_ref[1:2, part] = as_row(on_pos)
            loss = jnp.log(1.0 + product)
            loss_ref[b : b + 1] = jnp.sum(
                jnp.where(ids == order[...], loss, 0.0), axis=0, keepdims=True
            )


def split_store(b, total, keep_ref, send_ref):
    half = total.shape[0] // 2
    keep_ref[b * half : (b + 1) * half] = total[0:half]
    send_ref[b * half : (b + 1) * half] = total[half:]


def below_kernel(
    core_ref, own_ref, sib_ref, n1a_ref, n2a_ref, n1b_ref, n2b_ref, far_ref,
    e_ref, d_ref, sign_ref, f_ref, cols_ref, lanes_ref, loss_ref, keep_ref, send_ref,
):
    core = core_ref[0]

    @pl.when(core == 0)
    def _():
        rows = own_ref.shape[0]
        send_ref[rows : rows + 1, 0:rows] = loss_ref[1:2]
        chip = chip_rows(own_ref[...], sib_ref[...])
        near = near_rows(n1a_ref, n2a_ref, n1b_ref, n2b_ref)
        far = far_ref[...]
        zero = jnp.zeros((1, rows), F32)
        for b in range(2):
            part = slice(b * rows, (b + 1) * rows)
            on_neg = cols_ref[part, 0:1]
            on_pos = cols_ref[part, 1:2]
            lanes_neg = lanes_ref[0:1]
            lanes_pos = lanes_ref[1:2]
            d = d_ref[part]
            sign = sign_ref[part]
            columns = []
            for other in range(2):
                there = slice(other * rows, (other + 1) * rows)
                if other == b:
                    here = sign[:, there]
                    up = on_neg + lanes_neg[:, there]
                    down = on_pos + lanes_pos[:, there]
                    scale = jnp.where(here > 0.0, up, jnp.where(here < 0.0, -down, 0.0))
                elif b == 0:
                    scale = lanes_neg[:, there]
                else:
                    scale = on_neg
                columns.append((scale * d[:, there]).astype(BF16))
            total = jnp.dot(jnp.concatenate(columns, axis=1), chip, preferred_element_type=F32)
            total = total + jnp.dot(
                (on_neg * e_ref[part]).astype(BF16), near, preferred_element_type=F32
            )
            if b == 0:
                total = total + jnp.dot(
                    (on_neg * f_ref[...]).astype(BF16), far, preferred_element_type=F32
                )
            split_store(b, total, keep_ref, send_ref)


def above_kernel(
    core_ref, n1a_ref, n2a_ref, n1b_ref, n2b_ref, far_ref, e_ref, f_ref, on_near_ref, on_far_ref,
    keep_in, send_in,
    keep_ref, send_ref,
):
    core = core_ref[0]

    @pl.when(core == 1)
    def _():
        rows = far_ref.shape[0]
        near = near_rows(n1a_ref, n2a_ref, n1b_ref, n2b_ref)
        far = far_ref[...]
        for b in range(2):
            part = slice(b * rows, (b + 1) * rows)
            total = jnp.dot(
                (on_near_ref[...] * e_ref[part]).astype(BF16), near, preferred_element_type=F32
            )
            if b == 1:
                total = total + jnp.dot(
                    (on_far_ref[...] * f_ref[...]).astype(BF16), far, preferred_element_type=F32
                )
            split_store(b, total, keep_ref, send_ref)


def final_kernel(core_ref, x_ref, keep_ref, other_ref, losses_ref, grad_ref, loss_ref):
    rows = keep_ref.shape[0]
    loss_ref[...] = jnp.where(
        core_ref[0] == 0, losses_ref[0:1], other_ref[rows : rows + 1, 0:rows]
    )
    features = x_ref.shape[-1]
    half = keep_ref.shape[0] // 2
    for which in range(2):
        part = slice(which * half, (which + 1) * half)
        total = keep_ref[part] + other_ref[part]
        x = x_ref[:, which].astype(F32).reshape(half, features)
        inv = lax.rsqrt(jnp.sum(x * x, axis=1, keepdims=True) + 1e-06)
        u = x * inv
        grad = (total - u * jnp.sum(u * total, axis=1, keepdims=True)) * inv
        grad_ref[:, which] = grad.reshape(half // 8, 8, features).astype(BF16)


VMEM = pl.BlockSpec(memory_space=pltpu.VMEM)
SMEM = pl.BlockSpec(memory_space=pltpu.SMEM)


def shape(*size, dtype=F32):
    return jax.ShapeDtypeStruct(size, dtype)


def call(kernel, inputs, outputs, work, aliases=None):
    return pl.pallas_call(
        kernel,
        out_shape=outputs,
        in_specs=[SMEM if a.ndim == 1 else VMEM for a in inputs],
        out_specs=jax.tree.map(lambda _: VMEM, outputs),
        input_output_aliases=aliases or {},
        compiler_params=pltpu.CompilerParams(vmem_limit_bytes=LIMIT),
        cost_estimate=pl.CostEstimate(
            flops=int(work * 10**9), bytes_accessed=10**5, transcendentals=0
        ),
    )(*inputs)


def on_device(embeddings, order):
    rows, features = embeddings.shape
    peers = lax.axis_size(WHERE)
    per_peer = rows // peers
    half = rows // 2
    core = lax.axis_index("c").astype(jnp.int32).reshape(1)
    ring = lax.axis_size("y")

    def fetch_order(h):
        return lax.ppermute(order, ("c", "zh"), [(c * 2 + h, c) for c in range(2)])

    def along(value, moves):
        route = [(a * ring + y, b * ring + (y + s) % ring) for a, b, s in moves for y in range(ring)]
        return lax.ppermute(value, ("c", "y"), route)

    oa, ob = fetch_order(0), fetch_order(1)
    arrived = lax.all_to_all(
        embeddings.reshape(peers, per_peer, features), WHERE, 0, 0, tiled=True
    ).reshape(peers // 2, 2, per_peer, features)
    block = shape(rows, features, dtype=BF16)
    half_block = shape(half, features, dtype=BF16)

    own, one, two = call(
        pack_kernel, (core, arrived, oa, ob), (block, half_block, half_block), 0.01
    )
    straight = ((0, 0, 1), (1, 1, -1))
    across = ((1, 0, 1), (0, 1, -1))
    n1a = along(one, straight)
    n2a = along(two, across)
    n1b = along(two, straight)
    n2b = along(one, across)
    near = (n1a, n2a, n1b, n2b)
    far = along(call(relay_kernel, (n1a, n2a), block, 0.01), straight)
    sib = along(own, ((0, 1, 0), (1, 0, 0)))

    sign = call(mask_kernel, (core, oa, ob), shape(2 * rows, 2 * rows), 0.5)
    e, near_sums = call(
        near_kernel, (core, own, sib, *near), (shape(2 * rows, 2 * rows), shape(2 * rows, 8)), 0.8
    )
    d, own_sums = call(
        own_kernel, (core, own, sib, sign), (shape(2 * rows, 2 * rows), shape(2 * rows, 8)), 0.8
    )
    f, cols, lanes, losses, to_near, to_far = call(
        far_kernel,
        (core, own, sib, far, near_sums, own_sums, oa, ob),
        (
            shape(rows, rows),
            shape(2 * rows, 8),
            shape(2, 2 * rows),
            shape(2, rows),
            shape(1, 2 * rows),
            shape(1, rows),
        ),
        0.2,
    )
    on_near = along(to_near, ((0, 1, -1),))
    on_far = along(to_far, ((0, 1, -2),))
    half_grads = (shape(rows, features), shape(rows + 8, features))
    keep, send = call(
        below_kernel,
        (core, own, sib, *near, far, e, d, sign, f, cols, lanes, losses),
        half_grads,
        1.4,
    )
    keep, send = call(
        above_kernel,
        (core, *near, far, e, f, on_near, on_far, keep, send),
        half_grads,
        0.8,
        {10: 0, 11: 1},
    )
    other = along(send, ((0, 1, 0), (1, 0, 0)))
    grad, loss = call(
        final_kernel,
        (core, arrived, keep, other, losses),
        (shape(peers // 2, 2, per_peer, features, dtype=BF16), shape(1, rows)),
        0.01,
    )
    row_loss = lax.ppermute(
        loss, ("c", "zh"), [(c * 2 + h, h * 2 + c) for h in range(2) for c in range(2)]
    )
    sent_back = lax.all_to_all(
        grad.reshape(peers, per_peer, features), WHERE, 0, 0, tiled=True
    )
    return sent_back.reshape(rows, features), row_loss


def solution(mesh):
    dp, grp = mesh.devices.shape
    parts = Mesh(
        mesh.devices.reshape(dp // 8, 4, 2, grp // 2, 2), ("zl", "x", "c", "y", "zh")
    )
    placed = P(("zl", "x", "c", "y", "zh"), None)

    def step(embeddings, order):
        return on_device(embeddings, order)

    step = jax.shard_map(
        step, mesh=parts, in_specs=(placed, placed), out_specs=(placed, placed), check_vma=False
    )
    return step
```

```python
import jax
import jax.numpy as jnp
from jax import lax
from jax.experimental import pallas as pl
from jax.experimental.pallas import tpu as pltpu
from jax.sharding import Mesh
from jax.sharding import PartitionSpec as P


K = 16
gamma = 16.0
F32 = jnp.float32
BF16 = jnp.bfloat16
WHERE = ("zl", "x", "zh")
LIMIT = 20 * 2**20


def rows_by_rows(a, b):
    return lax.dot_general(a, b, (((1,), (1,)), ((), ())), preferred_element_type=F32)


def chip_rows(own, sib):
    half = own.shape[0] // 2
    return jnp.concatenate([own[0:half], sib[0:half], own[half:], sib[half:]], axis=0)


def as_row(column):
    return jnp.broadcast_to(column, (column.shape[0], 128)).T[0:1]


def over_rows(value):
    return jnp.sum(value, axis=0, keepdims=True)


def over_columns(value):
    return jnp.sum(value, axis=1, keepdims=True)


def arrived_rows(order_ref):
    rows = order_ref.shape[1]
    half = rows // 2
    i = lax.broadcasted_iota(jnp.int32, (rows, rows), 0)
    source = jnp.where(i < half, 0, 1)
    i = i - source * half
    return (i // 8) * 16 + source * 8 + i % 8 == order_ref[...]


def classes_kernel(core_ref, o0_ref, o1_ref, o2_ref, sign_ref):
    core = core_ref[0]
    rows = o0_ref.shape[1]
    slot = lax.broadcasted_iota(jnp.int32, (rows, 128), 0) // K
    table = jnp.where(lax.broadcasted_iota(jnp.int32, (rows, 128), 1) == slot, 1.0, 0.0)
    table = table.astype(BF16)
    diagonal = lax.broadcasted_iota(jnp.int32, (rows, rows), 0) == lax.broadcasted_iota(
        jnp.int32, (rows, rows), 1
    )

    def fill(b, ref):
        chosen = jnp.where(arrived_rows(ref), 1.0, 0.0).astype(BF16)
        hot = jnp.dot(chosen, table, preferred_element_type=F32).astype(BF16)
        sign_ref[b] = jnp.where(diagonal, 0.0, 1.0 - 2.0 * rows_by_rows(hot, hot))

    fill(0, o0_ref)
    fill(1, o1_ref)

    @pl.when(core == 1)
    def _():
        fill(2, o2_ref)


def pack_kernel(core_ref, x_ref, o0_ref, o1_ref, o2_ref, full_ref, one_ref, two_ref):
    core = core_ref[0]
    half = one_ref.shape[0]
    for which in range(2):
        x = x_ref[:, which].astype(F32).reshape(half, x_ref.shape[-1])
        inv = lax.rsqrt(jnp.sum(x * x, axis=1, keepdims=True) + 1e-06)
        unit = (x * inv).astype(BF16)
        full_ref[which * half : (which + 1) * half] = unit

        @pl.when(core == 1 - which)
        def _():
            one_ref[...] = unit

        @pl.when(core == which)
        def _():
            two_ref[...] = unit


def relay_kernel(own_ref, n1a_ref, n2a_ref, out_ref, both_ref):
    half = n1a_ref.shape[0]
    rows = 2 * half
    out_ref[0:half] = n2a_ref[...]
    out_ref[half:] = n1a_ref[...]
    both_ref[0:rows] = own_ref[...]
    both_ref[rows : rows + half] = n2a_ref[...]
    both_ref[rows + half :] = n1a_ref[...]


def signed_exp(sign, sim):
    e = jnp.exp(gamma * sign * sim)
    return e, jnp.where(sign < 0.0, e, 0.0), jnp.where(sign > 0.0, e, 0.0)


def factors(pos_sum, neg_sum):
    product = pos_sum * neg_sum
    weight = product / (1.0 + product)
    return gamma * weight / neg_sum, gamma * weight / pos_sum, jnp.log(1.0 + product)


def early_kernel(
    core_ref, own_ref, both_ref, n1a_ref, n2a_ref, n1b_ref, n2b_ref, sign_ref,
    e_ref, d_ref, cols_ref, lanes_ref,
):
    core = core_ref[0]
    rows = own_ref.shape[0]
    chip = chip_rows(own_ref[...], both_ref[0:rows])
    b_part = (n2b_ref[...], n1b_ref[...])
    a_part = (n2a_ref[...], n1a_ref[...])
    near = jnp.concatenate(b_part + a_part, axis=0)

    @pl.when(core == 0)
    def _():
        for b in range(2):
            part = slice(b * rows, (b + 1) * rows)
            e = jnp.exp(gamma * rows_by_rows(chip[part], near))
            e_ref[part] = e
            neg_sum = over_columns(e)
            for other in range(2):
                there = slice(other * rows, (other + 1) * rows)
                sim = rows_by_rows(chip[part], chip[there])
                if other == b:
                    d, pos, neg = signed_exp(sign_ref[b], sim)
                    neg_sum = neg_sum + over_columns(neg)
                    cols_ref[part, 0:1] = over_columns(pos)
                else:
                    d = jnp.exp(gamma * sim)
                    if b == 1:
                        neg_sum = neg_sum + over_columns(d)
                d_ref[part, there] = d
            cols_ref[part, 1:2] = neg_sum

    @pl.when(core == 1)
    def _():
        below = both_ref[rows:]
        for b in range(2):
            part = slice(b * rows, (b + 1) * rows)
            anchors = near[part]
            e = jnp.exp(gamma * rows_by_rows(chip, anchors))
            e_ref[:, part] = e
            _, pos, neg = signed_exp(sign_ref[b], rows_by_rows(anchors, anchors))
            third = near[rows:] if b == 0 else below
            lanes_ref[0:1, part] = over_rows(pos)
            lanes_ref[1:2, part] = (
                over_rows(e) + over_rows(neg) + over_rows(jnp.exp(gamma * rows_by_rows(third, anchors)))
            )


def late_kernel(
    core_ref, own_ref, both_ref, n1a_ref, n2a_ref, n1b_ref, n2b_ref, far_ref, sign_ref,
    e_ref, d_ref, cols_ref, lanes_ref, o0_ref, o1_ref, keep_ref, send_ref, loss_ref,
):
    core = core_ref[0]
    rows = own_ref.shape[0]
    chip = chip_rows(own_ref[...], both_ref[0:rows])
    near = jnp.concatenate([n2b_ref[...], n1b_ref[...], n2a_ref[...], n1a_ref[...]], axis=0)
    far = far_ref[...]

    @pl.when(core == 0)
    def _():
        f = jnp.exp(gamma * rows_by_rows(chip[0:rows], far))
        on_neg, on_pos, row_neg, row_pos = [], [], [], []
        for b, order_ref in enumerate((o0_ref, o1_ref)):
            part = slice(b * rows, (b + 1) * rows)
            neg_sum = cols_ref[part, 1:2]
            if b == 0:
                neg_sum = neg_sum + over_columns(f)
            up, down, loss = factors(cols_ref[part, 0:1], neg_sum)
            on_neg.append(up)
            on_pos.append(down)
            row_neg.append(as_row(up))
            row_pos.append(as_row(down))
            by_slot = over_rows(jnp.where(arrived_rows(order_ref), loss, 0.0))
            if b == 0:
                loss_ref[...] = by_slot
            else:
                send_ref[rows : rows + 1, 0:rows] = by_slot
        for b in range(2):
            part = slice(b * rows, (b + 1) * rows)
            total = jnp.dot(
                (on_neg[b] * e_ref[part]).astype(BF16), near, preferred_element_type=F32
            )
            for other in range(2):
                there = slice(other * rows, (other + 1) * rows)
                if other == b:
                    sign = sign_ref[b]
                    up = on_neg[b] + row_neg[b]
                    down = on_pos[b] + row_pos[b]
                    scale = jnp.where(sign > 0.0, up, jnp.where(sign < 0.0, -down, 0.0))
                elif b == 0:
                    scale = row_neg[1]
                else:
                    scale = on_neg[1]
                coef = (scale * d_ref[part, there]).astype(BF16)
                total = total + jnp.dot(coef, chip[there], preferred_element_type=F32)
            if b == 0:
                coef = (on_neg[0] * f).astype(BF16)
                total = total + jnp.dot(coef, far, preferred_element_type=F32)
            split_store(b, total, keep_ref, send_ref)

    @pl.when(core == 1)
    def _():
        f = jnp.exp(gamma * rows_by_rows(chip[rows:], far))
        _, pos, neg = signed_exp(sign_ref[2], rows_by_rows(far, far))
        others = jnp.exp(gamma * rows_by_rows(near, far))
        on_far, _, _ = factors(over_rows(pos), over_rows(f) + over_rows(neg) + over_rows(others))
        on_near, _, _ = factors(lanes_ref[0:1], lanes_ref[1:2])
        for b in range(2):
            part = slice(b * rows, (b + 1) * rows)
            coef = (on_near * e_ref[part]).astype(BF16)
            total = jnp.dot(coef, near, preferred_element_type=F32)
            if b == 1:
                coef = (on_far * f).astype(BF16)
                total = total + jnp.dot(coef, far, preferred_element_type=F32)
            split_store(b, total, keep_ref, send_ref)
        loss_ref[...] = jnp.zeros_like(loss_ref)


def split_store(b, total, keep_ref, send_ref):
    half = total.shape[0] // 2
    keep_ref[b * half : (b + 1) * half] = total[0:half]
    send_ref[b * half : (b + 1) * half] = total[half:]


def final_kernel(core_ref, x_ref, keep_ref, other_ref, losses_ref, grad_ref, loss_ref):
    rows = keep_ref.shape[0]
    loss_ref[...] = jnp.where(
        core_ref[0] == 0, losses_ref[...], other_ref[rows : rows + 1, 0:rows]
    )
    features = x_ref.shape[-1]
    half = keep_ref.shape[0] // 2
    for which in range(2):
        part = slice(which * half, (which + 1) * half)
        total = keep_ref[part] + other_ref[part]
        x = x_ref[:, which].astype(F32).reshape(half, features)
        inv = lax.rsqrt(jnp.sum(x * x, axis=1, keepdims=True) + 1e-06)
        u = x * inv
        grad = (total - u * jnp.sum(u * total, axis=1, keepdims=True)) * inv
        grad_ref[:, which] = grad.reshape(half // 8, 8, features).astype(BF16)


def copy_kernel(x_ref, out_ref):
    out_ref[...] = x_ref[...]


VMEM = pl.BlockSpec(memory_space=pltpu.VMEM)
SMEM = pl.BlockSpec(memory_space=pltpu.SMEM)


def shape(*size, dtype=F32):
    return jax.ShapeDtypeStruct(size, dtype)


def call(kernel, inputs, outputs, work, aliases=None):
    return pl.pallas_call(
        kernel,
        out_shape=outputs,
        in_specs=[SMEM if a.ndim == 1 else VMEM for a in inputs],
        out_specs=jax.tree.map(lambda _: VMEM, outputs),
        input_output_aliases=aliases or {},
        compiler_params=pltpu.CompilerParams(vmem_limit_bytes=LIMIT),
        cost_estimate=pl.CostEstimate(
            flops=int(work * 10**9), bytes_accessed=10**5, transcendentals=0
        ),
    )(*inputs)


def on_device(embeddings, order):
    rows, features = embeddings.shape
    peers = lax.axis_size(WHERE)
    per_peer = rows // peers
    half = rows // 2
    core = lax.axis_index("c").astype(jnp.int32).reshape(1)
    ring = lax.axis_size("y")

    def fetch_order(moves):
        route = [
            ((c * ring + y) * 2 + h, (core * ring + (y + s) % ring) * 2 + c)
            for h, core, s in moves
            for c in range(2)
            for y in range(ring)
        ]
        return lax.ppermute(order, ("c", "y", "zh"), route)

    def along(value, moves):
        route = [(a * ring + y, b * ring + (y + s) % ring) for a, b, s in moves for y in range(ring)]
        return lax.ppermute(value, ("c", "y"), route)

    o0 = fetch_order(((0, 0, 0), (1, 1, -1)))
    o1 = fetch_order(((1, 0, 0), (0, 1, -1)))
    o2 = fetch_order(((0, 1, -2),))
    arrived = lax.all_to_all(
        embeddings.reshape(peers, per_peer, features), WHERE, 0, 0, tiled=True
    ).reshape(peers // 2, 2, per_peer, features)
    block = shape(rows, features, dtype=BF16)
    half_block = shape(half, features, dtype=BF16)

    own, one, two = call(
        pack_kernel, (core, arrived, o0, o1, o2), (block, half_block, half_block), 0.01
    )
    straight = ((0, 0, 1), (1, 1, -1))
    across = ((1, 0, 1), (0, 1, -1))
    n1a = along(one, straight)
    n2a = along(two, across)
    n1b = along(two, straight)
    n2b = along(one, across)
    near = (n1a, n2a, n1b, n2b)
    relay, both = call(
        relay_kernel, (own, n1a, n2a), (block, shape(2 * rows, features, dtype=BF16)), 0.01
    )
    far = along(relay, straight)
    sib = along(both, ((0, 1, 0), (1, 0, 0)))

    sign = call(classes_kernel, (core, o0, o1, o2), shape(3, rows, rows), 0.5)
    e, d, cols, lanes = call(
        early_kernel,
        (core, own, sib, *near, sign),
        (
            shape(2 * rows, 2 * rows),
            shape(2 * rows, 2 * rows),
            shape(2 * rows, 8),
            shape(8, 2 * rows),
        ),
        1.2,
    )
    keep, send, losses = call(
        late_kernel,
        (core, own, sib, *near, far, sign, e, d, cols, lanes, o0, o1),
        (shape(rows, features), shape(rows + 8, features), shape(1, rows)),
        1.4,
    )
    other = along(send, ((0, 1, 0), (1, 0, 0)))
    grad, loss = call(
        final_kernel,
        (core, arrived, keep, other, losses),
        (shape(peers // 2, 2, per_peer, features, dtype=BF16), shape(1, rows)),
        0.01,
    )
    row_loss = lax.ppermute(
        loss, ("c", "zh"), [(c * 2 + h, h * 2 + c) for h in range(2) for c in range(2)]
    )
    row_loss = call(copy_kernel, (row_loss,), shape(1, rows), 0.001)
    sent_back = lax.all_to_all(
        grad.reshape(peers, per_peer, features), WHERE, 0, 0, tiled=True
    )
    return sent_back.reshape(rows, features), row_loss


def solution(mesh):
    dp, grp = mesh.devices.shape
    parts = Mesh(
        mesh.devices.reshape(dp // 8, 4, 2, grp // 2, 2), ("zl", "x", "c", "y", "zh")
    )
    placed = P(("zl", "x", "c", "y", "zh"), None)

    def step(embeddings, order):
        return on_device(embeddings, order)

    step = jax.shard_map(
        step, mesh=parts, in_specs=(placed, placed), out_specs=(placed, placed), check_vma=False
    )
    return step
```

```python
import jax
import jax.numpy as jnp
from jax import lax
from jax.experimental import pallas as pl
from jax.experimental.pallas import tpu as pltpu
from jax.sharding import Mesh
from jax.sharding import PartitionSpec as P


K = 16
gamma = 16.0
F32 = jnp.float32
BF16 = jnp.bfloat16
WHERE = ("zl", "x", "zh")
LIMIT = 20 * 2**20


def rows_by_rows(a, b):
    return lax.dot_general(a, b, (((1,), (1,)), ((), ())), preferred_element_type=F32)


def chip_rows(own, sib):
    half = own.shape[0] // 2
    return jnp.concatenate([own[0:half], sib[0:half], own[half:], sib[half:]], axis=0)


def as_row(column):
    return jnp.broadcast_to(column, (column.shape[0], 128)).T[0:1]


def over_rows(value):
    return jnp.sum(value, axis=0, keepdims=True)


def over_columns(value):
    return jnp.sum(value, axis=1, keepdims=True)


def arrived_rows(order_ref):
    rows = order_ref.shape[1]
    half = rows // 2
    i = lax.broadcasted_iota(jnp.int32, (rows, rows), 0)
    source = jnp.where(i < half, 0, 1)
    i = i - source * half
    return (i // 8) * 16 + source * 8 + i % 8 == order_ref[...]


def classes_kernel(core_ref, o0_ref, o1_ref, o2_ref, sign_ref):
    core = core_ref[0]
    rows = o0_ref.shape[1]
    slot = lax.broadcasted_iota(jnp.int32, (rows, 128), 0) // K
    table = jnp.where(lax.broadcasted_iota(jnp.int32, (rows, 128), 1) == slot, 1.0, 0.0)
    table = table.astype(BF16)
    diagonal = lax.broadcasted_iota(jnp.int32, (rows, rows), 0) == lax.broadcasted_iota(
        jnp.int32, (rows, rows), 1
    )

    def fill(b, ref):
        chosen = jnp.where(arrived_rows(ref), 1.0, 0.0).astype(BF16)
        hot = jnp.dot(chosen, table, preferred_element_type=F32).astype(BF16)
        sign_ref[b] = jnp.where(diagonal, 0.0, 1.0 - 2.0 * rows_by_rows(hot, hot))

    fill(0, o0_ref)
    fill(1, o1_ref)

    @pl.when(core == 1)
    def _():
        fill(2, o2_ref)


def pack_kernel(core_ref, x_ref, full_ref, one_ref, two_ref):
    core = core_ref[0]
    half = one_ref.shape[0]
    for which in range(2):
        x = x_ref[:, which].astype(F32).reshape(half, x_ref.shape[-1])
        inv = lax.rsqrt(jnp.sum(x * x, axis=1, keepdims=True) + 1e-06)
        unit = (x * inv).astype(BF16)
        full_ref[which * half : (which + 1) * half] = unit

        @pl.when(core == 1 - which)
        def _():
            one_ref[...] = unit

        @pl.when(core == which)
        def _():
            two_ref[...] = unit


def relay_kernel(own_ref, n1a_ref, n2a_ref, out_ref, both_ref):
    half = n1a_ref.shape[0]
    rows = 2 * half
    out_ref[0:half] = n2a_ref[...]
    out_ref[half:] = n1a_ref[...]
    both_ref[0:rows] = own_ref[...]
    both_ref[rows : rows + half] = n2a_ref[...]
    both_ref[rows + half :] = n1a_ref[...]


def signed_exp(sign, sim):
    e = jnp.exp(gamma * sign * sim)
    return e, jnp.where(sign < 0.0, e, 0.0), jnp.where(sign > 0.0, e, 0.0)


def factors(pos_sum, neg_sum):
    product = pos_sum * neg_sum
    weight = product / (1.0 + product)
    return gamma * weight / neg_sum, gamma * weight / pos_sum, jnp.log(1.0 + product)


def early_kernel(
    core_ref, own_ref, both_ref, n1a_ref, n2a_ref, n1b_ref, n2b_ref, sign_ref,
    e_ref, d_ref, cols_ref, lanes_ref,
):
    core = core_ref[0]
    rows = own_ref.shape[0]
    chip = chip_rows(own_ref[...], both_ref[0:rows])
    b_part = (n2b_ref[...], n1b_ref[...])
    a_part = (n2a_ref[...], n1a_ref[...])
    near = jnp.concatenate(b_part + a_part, axis=0)

    @pl.when(core == 0)
    def _():
        for b in range(2):
            part = slice(b * rows, (b + 1) * rows)
            e = jnp.exp(gamma * rows_by_rows(chip[part], near))
            e_ref[part] = e
            neg_sum = over_columns(e)
            for other in range(2):
                there = slice(other * rows, (other + 1) * rows)
                sim = rows_by_rows(chip[part], chip[there])
                if other == b:
                    d, pos, neg = signed_exp(sign_ref[b], sim)
                    neg_sum = neg_sum + over_columns(neg)
                    cols_ref[part, 0:1] = over_columns(pos)
                else:
                    d = jnp.exp(gamma * sim)
                    if b == 1:
                        neg_sum = neg_sum + over_columns(d)
                d_ref[part, there] = d
            cols_ref[part, 1:2] = neg_sum

    @pl.when(core == 1)
    def _():
        below = both_ref[rows:]
        for b in range(2):
            part = slice(b * rows, (b + 1) * rows)
            anchors = near[part]
            e = jnp.exp(gamma * rows_by_rows(chip, anchors))
            e_ref[:, part] = e
            _, pos, neg = signed_exp(sign_ref[b], rows_by_rows(anchors, anchors))
            third = near[rows:] if b == 0 else below
            lanes_ref[0:1, part] = over_rows(pos)
            lanes_ref[1:2, part] = (
                over_rows(e) + over_rows(neg) + over_rows(jnp.exp(gamma * rows_by_rows(third, anchors)))
            )


def late_kernel(
    core_ref, own_ref, both_ref, n1a_ref, n2a_ref, n1b_ref, n2b_ref, far_ref, sign_ref,
    e_ref, d_ref, cols_ref, lanes_ref, o0_ref, o1_ref, keep_ref, send_ref, loss_ref,
):
    core = core_ref[0]
    rows = own_ref.shape[0]
    chip = chip_rows(own_ref[...], both_ref[0:rows])
    near = jnp.concatenate([n2b_ref[...], n1b_ref[...], n2a_ref[...], n1a_ref[...]], axis=0)
    far = far_ref[...]

    @pl.when(core == 0)
    def _():
        f = jnp.exp(gamma * rows_by_rows(chip[0:rows], far))
        on_neg, on_pos, row_neg, row_pos = [], [], [], []
        for b, order_ref in enumerate((o0_ref, o1_ref)):
            part = slice(b * rows, (b + 1) * rows)
            neg_sum = cols_ref[part, 1:2]
            if b == 0:
                neg_sum = neg_sum + over_columns(f)
            up, down, loss = factors(cols_ref[part, 0:1], neg_sum)
            on_neg.append(up)
            on_pos.append(down)
            row_neg.append(as_row(up))
            row_pos.append(as_row(down))
            by_slot = over_rows(jnp.where(arrived_rows(order_ref), loss, 0.0))
            if b == 0:
                loss_ref[...] = by_slot
            else:
                send_ref[rows : rows + 1, 0:rows] = by_slot
        for b in range(2):
            part = slice(b * rows, (b + 1) * rows)
            total = jnp.dot(
                (on_neg[b] * e_ref[part]).astype(BF16), near, preferred_element_type=F32
            )
            for other in range(2):
                there = slice(other * rows, (other + 1) * rows)
                if other == b:
                    sign = sign_ref[b]
                    up = on_neg[b] + row_neg[b]
                    down = on_pos[b] + row_pos[b]
                    scale = jnp.where(sign > 0.0, up, jnp.where(sign < 0.0, -down, 0.0))
                elif b == 0:
                    scale = row_neg[1]
                else:
                    scale = on_neg[1]
                coef = (scale * d_ref[part, there]).astype(BF16)
                total = total + jnp.dot(coef, chip[there], preferred_element_type=F32)
            if b == 0:
                coef = (on_neg[0] * f).astype(BF16)
                total = total + jnp.dot(coef, far, preferred_element_type=F32)
            split_store(b, total, keep_ref, send_ref)

    @pl.when(core == 1)
    def _():
        f = jnp.exp(gamma * rows_by_rows(chip[rows:], far))
        _, pos, neg = signed_exp(sign_ref[2], rows_by_rows(far, far))
        others = jnp.exp(gamma * rows_by_rows(near, far))
        on_far, _, _ = factors(over_rows(pos), over_rows(f) + over_rows(neg) + over_rows(others))
        on_near, _, _ = factors(lanes_ref[0:1], lanes_ref[1:2])
        for b in range(2):
            part = slice(b * rows, (b + 1) * rows)
            coef = (on_near * e_ref[part]).astype(BF16)
            total = jnp.dot(coef, near, preferred_element_type=F32)
            if b == 1:
                coef = (on_far * f).astype(BF16)
                total = total + jnp.dot(coef, far, preferred_element_type=F32)
            split_store(b, total, keep_ref, send_ref)
        loss_ref[...] = jnp.zeros_like(loss_ref)


def split_store(b, total, keep_ref, send_ref):
    half = total.shape[0] // 2
    keep_ref[b * half : (b + 1) * half] = total[0:half]
    send_ref[b * half : (b + 1) * half] = total[half:]


def final_kernel(core_ref, x_ref, keep_ref, other_ref, losses_ref, grad_ref, loss_ref):
    rows = keep_ref.shape[0]
    loss_ref[...] = jnp.where(
        core_ref[0] == 0, losses_ref[...], other_ref[rows : rows + 1, 0:rows]
    )
    features = x_ref.shape[-1]
    half = keep_ref.shape[0] // 2
    for which in range(2):
        part = slice(which * half, (which + 1) * half)
        total = keep_ref[part] + other_ref[part]
        x = x_ref[:, which].astype(F32).reshape(half, features)
        inv = lax.rsqrt(jnp.sum(x * x, axis=1, keepdims=True) + 1e-06)
        u = x * inv
        grad = (total - u * jnp.sum(u * total, axis=1, keepdims=True)) * inv
        grad_ref[:, which] = grad.reshape(half // 8, 8, features).astype(BF16)


def copy_kernel(x_ref, out_ref):
    out_ref[...] = x_ref[...]


VMEM = pl.BlockSpec(memory_space=pltpu.VMEM)
SMEM = pl.BlockSpec(memory_space=pltpu.SMEM)


def shape(*size, dtype=F32):
    return jax.ShapeDtypeStruct(size, dtype)


def call(kernel, inputs, outputs, work, aliases=None):
    return pl.pallas_call(
        kernel,
        out_shape=outputs,
        in_specs=[SMEM if a.ndim == 1 else VMEM for a in inputs],
        out_specs=jax.tree.map(lambda _: VMEM, outputs),
        input_output_aliases=aliases or {},
        compiler_params=pltpu.CompilerParams(vmem_limit_bytes=LIMIT),
        cost_estimate=pl.CostEstimate(
            flops=int(work * 10**9), bytes_accessed=10**5, transcendentals=0
        ),
    )(*inputs)


def on_device(embeddings, order):
    rows, features = embeddings.shape
    peers = lax.axis_size(WHERE)
    per_peer = rows // peers
    half = rows // 2
    core = lax.axis_index("c").astype(jnp.int32).reshape(1)
    ring = lax.axis_size("y")

    def fetch_order(moves):
        route = [
            ((c * ring + y) * 2 + h, (core * ring + (y + s) % ring) * 2 + c)
            for h, core, s in moves
            for c in range(2)
            for y in range(ring)
        ]
        return lax.ppermute(order, ("c", "y", "zh"), route)

    def along(value, moves):
        route = [(a * ring + y, b * ring + (y + s) % ring) for a, b, s in moves for y in range(ring)]
        return lax.ppermute(value, ("c", "y"), route)

    o0 = fetch_order(((0, 0, 0), (1, 1, -1)))
    o1 = fetch_order(((1, 0, 0), (0, 1, -1)))
    o2 = fetch_order(((0, 1, -2),))
    arrived = lax.all_to_all(
        embeddings.reshape(peers, per_peer, features), WHERE, 0, 0, tiled=True
    ).reshape(peers // 2, 2, per_peer, features)
    block = shape(rows, features, dtype=BF16)
    half_block = shape(half, features, dtype=BF16)

    own, one, two = call(pack_kernel, (core, arrived), (block, half_block, half_block), 0.01)
    straight = ((0, 0, 1), (1, 1, -1))
    across = ((1, 0, 1), (0, 1, -1))
    n1a = along(one, straight)
    n2a = along(two, across)
    n1b = along(two, straight)
    n2b = along(one, across)
    near = (n1a, n2a, n1b, n2b)
    relay, both = call(
        relay_kernel, (own, n1a, n2a), (block, shape(2 * rows, features, dtype=BF16)), 0.01
    )
    far = along(relay, straight)
    sib = along(both, ((0, 1, 0), (1, 0, 0)))

    sign = call(classes_kernel, (core, o0, o1, o2), shape(3, rows, rows), 0.5)
    e, d, cols, lanes = call(
        early_kernel,
        (core, own, sib, *near, sign),
        (
            shape(2 * rows, 2 * rows),
            shape(2 * rows, 2 * rows),
            shape(2 * rows, 8),
            shape(8, 2 * rows),
        ),
        1.2,
    )
    keep, send, losses = call(
        late_kernel,
        (core, own, sib, *near, far, sign, e, d, cols, lanes, o0, o1),
        (shape(rows, features), shape(rows + 8, features), shape(1, rows)),
        1.4,
    )
    other = along(send, ((0, 1, 0), (1, 0, 0)))
    grad, loss = call(
        final_kernel,
        (core, arrived, keep, other, losses),
        (shape(peers // 2, 2, per_peer, features, dtype=BF16), shape(1, rows)),
        0.01,
    )
    row_loss = lax.ppermute(
        loss, ("c", "zh"), [(c * 2 + h, h * 2 + c) for h in range(2) for c in range(2)]
    )
    row_loss = call(copy_kernel, (row_loss,), shape(1, rows), 0.001)
    sent_back = lax.all_to_all(
        grad.reshape(peers, per_peer, features), WHERE, 0, 0, tiled=True
    )
    return sent_back.reshape(rows, features), row_loss


def solution(mesh):
    dp, grp = mesh.devices.shape
    parts = Mesh(
        mesh.devices.reshape(dp // 8, 4, 2, grp // 2, 2), ("zl", "x", "c", "y", "zh")
    )
    placed = P(("zl", "x", "c", "y", "zh"), None)

    def step(embeddings, order):
        return on_device(embeddings, order)

    step = jax.shard_map(
        step, mesh=parts, in_specs=(placed, placed), out_specs=(placed, placed), check_vma=False
    )
    return step
```

```python
import jax
import jax.numpy as jnp
from jax import lax
from jax.experimental import pallas as pl
from jax.experimental.pallas import tpu as pltpu
from jax.sharding import Mesh
from jax.sharding import PartitionSpec as P


K = 16
gamma = 16.0
F32 = jnp.float32
BF16 = jnp.bfloat16
WHERE = ("zl", "x", "zh")
LIMIT = 20 * 2**20


def rows_by_rows(a, b):
    return lax.dot_general(a, b, (((1,), (1,)), ((), ())), preferred_element_type=F32)


def as_row(column):
    return jnp.broadcast_to(column, (column.shape[0], 128)).T[0:1]


def over_rows(value):
    return jnp.sum(value, axis=0, keepdims=True)


def over_columns(value):
    return jnp.sum(value, axis=1, keepdims=True)


def arrived_rows(order_ref):
    rows = order_ref.shape[1]
    half = rows // 2
    i = lax.broadcasted_iota(jnp.int32, (rows, rows), 0)
    source = jnp.where(i < half, 0, 1)
    i = i - source * half
    return (i // 8) * 16 + source * 8 + i % 8 == order_ref[...]


def classes_kernel(core_ref, o0_ref, o1_ref, o2_ref, sign_ref):
    core = core_ref[0]
    rows = o0_ref.shape[1]
    slot = lax.broadcasted_iota(jnp.int32, (rows, 128), 0) // K
    table = jnp.where(lax.broadcasted_iota(jnp.int32, (rows, 128), 1) == slot, 1.0, 0.0)
    table = table.astype(BF16)
    diagonal = lax.broadcasted_iota(jnp.int32, (rows, rows), 0) == lax.broadcasted_iota(
        jnp.int32, (rows, rows), 1
    )

    def fill(b, ref):
        chosen = jnp.where(arrived_rows(ref), 1.0, 0.0).astype(BF16)
        hot = jnp.dot(chosen, table, preferred_element_type=F32).astype(BF16)
        sign_ref[b] = jnp.where(diagonal, 0.0, 1.0 - 2.0 * rows_by_rows(hot, hot))

    fill(0, o0_ref)
    fill(1, o1_ref)

    @pl.when(core == 1)
    def _():
        fill(2, o2_ref)


def pack_kernel(x_ref, full_ref):
    half = full_ref.shape[0] // 2
    for which in range(2):
        x = x_ref[:, which].astype(F32).reshape(half, x_ref.shape[-1])
        inv = lax.rsqrt(jnp.sum(x * x, axis=1, keepdims=True) + 1e-06)
        full_ref[which * half : (which + 1) * half] = (x * inv).astype(BF16)


def merge_kernel(core_ref, own_ref, sib_ref, first_ref, second_ref):
    half = own_ref.shape[0] // 2
    a, b = slice(0, half), slice(half, 2 * half)

    @pl.when(core_ref[0] == 0)
    def _():
        first_ref[a], first_ref[b] = own_ref[b], sib_ref[b]
        second_ref[a], second_ref[b] = own_ref[a], sib_ref[a]

    @pl.when(core_ref[0] == 1)
    def _():
        first_ref[a], first_ref[b] = sib_ref[a], own_ref[a]
        second_ref[a], second_ref[b] = sib_ref[b], own_ref[b]


def signed_exp(sign, sim):
    e = jnp.exp(gamma * sign * sim)
    return e, jnp.where(sign < 0.0, e, 0.0), jnp.where(sign > 0.0, e, 0.0)


def factors(pos_sum, neg_sum):
    product = pos_sum * neg_sum
    weight = product / (1.0 + product)
    return gamma * weight / neg_sum, gamma * weight / pos_sum, jnp.log(1.0 + product)


def scaled_dot(scale, e, rows):
    return jnp.dot((scale * e).astype(BF16), rows, preferred_element_type=F32)


def paired(sign, up, down, row_up, row_down, e):
    scale = jnp.where(sign < 0.0, -(down + row_down), 0.0)
    return (jnp.where(sign > 0.0, up + row_up, scale) * e).astype(BF16)


def split_store(core, which, total, keep_ref, send_ref):
    half = total.shape[0] // 2
    mine = slice(core * half, (core + 1) * half)
    other = slice((1 - core) * half, (2 - core) * half)
    place = slice(which * half, (which + 1) * half)
    keep_ref[place] = total[mine]
    send_ref[place] = total[other]


def pairs_kernel(core_ref, first_ref, second_ref, sign_ref, d_ref, sums_ref):
    @pl.when(core_ref[0] == 0)
    def _():
        rows = first_ref.shape[0]
        a, b = slice(0, rows), slice(rows, 2 * rows)
        chip_a, chip_b = second_ref[...], first_ref[...]
        d_ref[a, b] = jnp.exp(gamma * rows_by_rows(chip_a, chip_b))
        d_ba = jnp.exp(gamma * rows_by_rows(chip_b, chip_a))
        d_ref[b, a] = d_ba
        for part, chip, sign in ((a, chip_a, sign_ref[0]), (b, chip_b, sign_ref[1])):
            d, pos, neg = signed_exp(sign, rows_by_rows(chip, chip))
            d_ref[part, part] = d
            total = over_columns(neg)
            if part is b:
                total = total + over_columns(d_ba)
            sums_ref[part, 0:1] = over_columns(pos)
            sums_ref[part, 1:2] = total


def early_kernel(
    core_ref, first_ref, second_ref, na_ref, nb_ref, third_ref, sign_ref, d_ref, own_sums_ref, o1_ref,
    e_ref, sums_ref, acc_ref, keep_ref, send_ref,
):
    core = core_ref[0]
    rows = first_ref.shape[0]
    a, b = slice(0, rows), slice(rows, 2 * rows)
    near = jnp.concatenate([nb_ref[...], na_ref[...]], axis=0)

    @pl.when(core == 0)
    def _():
        chip_a, chip_b = second_ref[...], first_ref[...]
        e_b = jnp.exp(gamma * rows_by_rows(chip_b, near))
        neg_sum = own_sums_ref[b, 1:2] + over_columns(e_b)
        up, down, loss = factors(own_sums_ref[b, 0:1], neg_sum)
        row_up = as_row(up)
        send_ref[rows : rows + 1, 0:rows] = over_rows(jnp.where(arrived_rows(o1_ref), loss, 0.0))
        coef = paired(sign_ref[1], up, down, row_up, as_row(down), d_ref[b, b])
        total = jnp.dot(coef, chip_b, preferred_element_type=F32)
        total = total + scaled_dot(up, e_b, near) + scaled_dot(up, d_ref[b, a], chip_a)
        split_store(0, 1, total, keep_ref, send_ref)
        acc_ref[...] = scaled_dot(row_up, d_ref[a, b], chip_b)
        e_a = jnp.exp(gamma * rows_by_rows(chip_a, near))
        e_ref[a] = e_a
        sums_ref[:, 0:1] = own_sums_ref[a, 0:1]
        sums_ref[:, 1:2] = own_sums_ref[a, 1:2] + over_columns(e_a)

    @pl.when(core == 1)
    def _():
        chip = jnp.concatenate([first_ref[...], second_ref[...]], axis=0)
        scale = []
        for part, third, sign in ((a, near[b], sign_ref[0]), (b, third_ref[...], sign_ref[1])):
            anchors = near[part]
            e = jnp.exp(gamma * rows_by_rows(chip, anchors))
            e_ref[:, part] = e
            _, pos, neg = signed_exp(sign, rows_by_rows(anchors, anchors))
            others = jnp.exp(gamma * rows_by_rows(third, anchors))
            up, _, _ = factors(over_rows(pos), over_rows(e) + over_rows(neg) + over_rows(others))
            scale.append(up)
        scale = jnp.concatenate(scale, axis=1)
        split_store(1, 0, scaled_dot(scale, e_ref[a], near), keep_ref, send_ref)
        acc_ref[...] = scaled_dot(scale, e_ref[b], near)


def late_kernel(
    core_ref, first_ref, second_ref, na_ref, nb_ref, far_ref, sign_ref,
    e_ref, d_ref, sums_ref, acc_ref, o0_ref, keep_in, send_in, keep_ref, send_ref, loss_ref,
):
    core = core_ref[0]
    rows = first_ref.shape[0]
    a = slice(0, rows)
    near = jnp.concatenate([nb_ref[...], na_ref[...]], axis=0)
    far = far_ref[...]

    @pl.when(core == 0)
    def _():
        chip_a = second_ref[...]
        f = jnp.exp(gamma * rows_by_rows(chip_a, far))
        up, down, loss = factors(sums_ref[:, 0:1], sums_ref[:, 1:2] + over_columns(f))
        coef = paired(sign_ref[0], up, down, as_row(up), as_row(down), d_ref[a, a])
        total = acc_ref[...] + jnp.dot(coef, chip_a, preferred_element_type=F32)
        total = total + scaled_dot(up, e_ref[a], near) + scaled_dot(up, f, far)
        split_store(0, 0, total, keep_ref, send_ref)
        loss_ref[...] = over_rows(jnp.where(arrived_rows(o0_ref), loss, 0.0))

    @pl.when(core == 1)
    def _():
        f = jnp.exp(gamma * rows_by_rows(second_ref[...], far))
        _, pos, neg = signed_exp(sign_ref[2], rows_by_rows(far, far))
        others = jnp.exp(gamma * rows_by_rows(near, far))
        up, _, _ = factors(over_rows(pos), over_rows(f) + over_rows(neg) + over_rows(others))
        split_store(1, 1, acc_ref[...] + scaled_dot(up, f, far), keep_ref, send_ref)
        loss_ref[...] = jnp.zeros_like(loss_ref)


def final_kernel(core_ref, x_ref, keep_ref, other_ref, losses_ref, grad_ref, loss_ref):
    rows = keep_ref.shape[0]
    loss_ref[...] = jnp.where(
        core_ref[0] == 0, losses_ref[...], other_ref[rows : rows + 1, 0:rows]
    )
    features = x_ref.shape[-1]
    half = keep_ref.shape[0] // 2
    for which in range(2):
        part = slice(which * half, (which + 1) * half)
        total = keep_ref[part] + other_ref[part]
        x = x_ref[:, which].astype(F32).reshape(half, features)
        inv = lax.rsqrt(jnp.sum(x * x, axis=1, keepdims=True) + 1e-06)
        u = x * inv
        grad = (total - u * jnp.sum(u * total, axis=1, keepdims=True)) * inv
        grad_ref[:, which] = grad.reshape(half // 8, 8, features).astype(BF16)


def copy_kernel(x_ref, out_ref):
    out_ref[...] = x_ref[...]


VMEM = pl.BlockSpec(memory_space=pltpu.VMEM)
SMEM = pl.BlockSpec(memory_space=pltpu.SMEM)


def shape(*size, dtype=F32):
    return jax.ShapeDtypeStruct(size, dtype)


def call(kernel, inputs, outputs, work, aliases=None):
    return pl.pallas_call(
        kernel,
        out_shape=outputs,
        in_specs=[SMEM if a.ndim == 1 else VMEM for a in inputs],
        out_specs=jax.tree.map(lambda _: VMEM, outputs),
        input_output_aliases=aliases or {},
        compiler_params=pltpu.CompilerParams(vmem_limit_bytes=LIMIT),
        cost_estimate=pl.CostEstimate(
            flops=int(work * 10**9), bytes_accessed=10**5, transcendentals=0
        ),
    )(*inputs)


def on_device(embeddings, order):
    rows, features = embeddings.shape
    peers = lax.axis_size(WHERE)
    per_peer = rows // peers
    core = lax.axis_index("c").astype(jnp.int32).reshape(1)
    ring = lax.axis_size("y")

    def fetch_order(moves):
        route = [
            ((c * ring + y) * 2 + h, (core * ring + (y + s) % ring) * 2 + c)
            for h, core, s in moves
            for c in range(2)
            for y in range(ring)
        ]
        return lax.ppermute(order, ("c", "y", "zh"), route)

    def along(value, moves):
        route = [(a * ring + y, b * ring + (y + s) % ring) for a, b, s in moves for y in range(ring)]
        return lax.ppermute(value, ("c", "y"), route)

    o0 = fetch_order(((0, 0, 0), (1, 1, -1)))
    o1 = fetch_order(((1, 0, 0), (0, 1, -1)))
    o2 = fetch_order(((0, 1, -2),))
    arrived = lax.all_to_all(
        embeddings.reshape(peers, per_peer, features), WHERE, 0, 0, tiled=True
    ).reshape(peers // 2, 2, per_peer, features)
    block = shape(rows, features, dtype=BF16)
    chip_pairs = shape(2 * rows, 2 * rows)

    own = call(pack_kernel, (arrived,), block, 0.01)
    swapped = ((0, 1, 0), (1, 0, 0))
    onward = ((0, 0, 1), (1, 1, -1))
    sib = along(own, swapped)
    first, second = call(merge_kernel, (core, own, sib), (block, block), 0.01)
    na = along(first, onward)
    nb = along(second, onward)
    far = along(na, onward)
    third = along(na, swapped)

    sign = call(classes_kernel, (core, o0, o1, o2), shape(3, rows, rows), 0.5)
    d, own_sums = call(
        pairs_kernel, (core, first, second, sign), (chip_pairs, shape(2 * rows, 8)), 0.6
    )
    half_grads = (shape(rows, features), shape(rows + 8, features))
    e, sums, acc, keep, send = call(
        early_kernel,
        (core, first, second, na, nb, third, sign, d, own_sums, o1),
        (chip_pairs, shape(rows, 8), shape(rows, features), *half_grads),
        2.0,
    )
    keep, send, losses = call(
        late_kernel,
        (core, first, second, na, nb, far, sign, e, d, sums, acc, o0, keep, send),
        (*half_grads, shape(1, rows)),
        0.8,
        {12: 0, 13: 1},
    )
    other = along(send, swapped)
    grad, loss = call(
        final_kernel,
        (core, arrived, keep, other, losses),
        (shape(peers // 2, 2, per_peer, features, dtype=BF16), shape(1, rows)),
        0.01,
    )
    row_loss = lax.ppermute(
        loss, ("c", "zh"), [(c * 2 + h, h * 2 + c) for h in range(2) for c in range(2)]
    )
    row_loss = call(copy_kernel, (row_loss,), shape(1, rows), 0.001)
    sent_back = lax.all_to_all(
        grad.reshape(peers, per_peer, features), WHERE, 0, 0, tiled=True
    )
    return sent_back.reshape(rows, features), row_loss


def solution(mesh):
    dp, grp = mesh.devices.shape
    parts = Mesh(
        mesh.devices.reshape(dp // 8, 4, 2, grp // 2, 2), ("zl", "x", "c", "y", "zh")
    )
    placed = P(("zl", "x", "c", "y", "zh"), None)

    def step(embeddings, order):
        return on_device(embeddings, order)

    step = jax.shard_map(
        step, mesh=parts, in_specs=(placed, placed), out_specs=(placed, placed), check_vma=False
    )
    return step
```

```python
import jax
import jax.numpy as jnp
from jax import lax
from jax.experimental import pallas as pl
from jax.experimental.pallas import tpu as pltpu
from jax.sharding import Mesh
from jax.sharding import PartitionSpec as P


K = 16
gamma = 16.0
F32 = jnp.float32
BF16 = jnp.bfloat16
WHERE = ("zl", "x", "zh")
LIMIT = 20 * 2**20


def rows_by_rows(a, b):
    return lax.dot_general(a, b, (((1,), (1,)), ((), ())), preferred_element_type=F32)


def chip_rows(own, sib):
    half = own.shape[0] // 2
    return jnp.concatenate([own[0:half], sib[0:half], own[half:], sib[half:]], axis=0)


def as_row(column):
    return jnp.broadcast_to(column, (column.shape[0], 128)).T[0:1]


def over_rows(value):
    return jnp.sum(value, axis=0, keepdims=True)


def over_columns(value):
    return jnp.sum(value, axis=1, keepdims=True)


def arrived_rows(order_ref):
    rows = order_ref.shape[1]
    half = rows // 2
    i = lax.broadcasted_iota(jnp.int32, (rows, rows), 0)
    source = jnp.where(i < half, 0, 1)
    i = i - source * half
    return (i // 8) * 16 + source * 8 + i % 8 == order_ref[...]


def classes_kernel(core_ref, o0_ref, o1_ref, o2_ref, sign_ref):
    core = core_ref[0]
    rows = o0_ref.shape[1]
    slot = lax.broadcasted_iota(jnp.int32, (rows, 128), 0) // K
    table = jnp.where(lax.broadcasted_iota(jnp.int32, (rows, 128), 1) == slot, 1.0, 0.0)
    table = table.astype(BF16)
    diagonal = lax.broadcasted_iota(jnp.int32, (rows, rows), 0) == lax.broadcasted_iota(
        jnp.int32, (rows, rows), 1
    )

    def fill(b, ref):
        chosen = jnp.where(arrived_rows(ref), 1.0, 0.0).astype(BF16)
        hot = jnp.dot(chosen, table, preferred_element_type=F32).astype(BF16)
        sign_ref[b] = jnp.where(diagonal, 0.0, 1.0 - 2.0 * rows_by_rows(hot, hot))

    fill(0, o0_ref)
    fill(1, o1_ref)

    @pl.when(core == 1)
    def _():
        fill(2, o2_ref)


def pack_kernel(core_ref, x_ref, full_ref, one_ref, two_ref):
    core = core_ref[0]
    half = one_ref.shape[0]
    for which in range(2):
        x = x_ref[:, which].astype(F32).reshape(half, x_ref.shape[-1])
        inv = lax.rsqrt(jnp.sum(x * x, axis=1, keepdims=True) + 1e-06)
        unit = (x * inv).astype(BF16)
        full_ref[which * half : (which + 1) * half] = unit

        @pl.when(core == 1 - which)
        def _():
            one_ref[...] = unit

        @pl.when(core == which)
        def _():
            two_ref[...] = unit


def relay_kernel(own_ref, n1a_ref, n2a_ref, out_ref, both_ref):
    half = n1a_ref.shape[0]
    rows = 2 * half
    out_ref[0:half] = n2a_ref[...]
    out_ref[half:] = n1a_ref[...]
    both_ref[0:rows] = own_ref[...]
    both_ref[rows : rows + half] = n2a_ref[...]
    both_ref[rows + half :] = n1a_ref[...]


def signed_exp(sign, sim):
    e = jnp.exp(gamma * sign * sim)
    return e, jnp.where(sign < 0.0, e, 0.0), jnp.where(sign > 0.0, e, 0.0)


def factors(pos_sum, neg_sum):
    product = pos_sum * neg_sum
    weight = product / (1.0 + product)
    return gamma * weight / neg_sum, gamma * weight / pos_sum, jnp.log(1.0 + product)


def scaled_dot(scale, e, rows):
    return jnp.dot((scale * e).astype(BF16), rows, preferred_element_type=F32)


def paired(sign, up, down, row_up, row_down, e):
    scale = jnp.where(sign < 0.0, -(down + row_down), 0.0)
    return (jnp.where(sign > 0.0, up + row_up, scale) * e).astype(BF16)


def split_store(b, total, keep_ref, send_ref):
    half = total.shape[0] // 2
    keep_ref[b * half : (b + 1) * half] = total[0:half]
    send_ref[b * half : (b + 1) * half] = total[half:]


def early_kernel(
    core_ref, own_ref, both_ref, n1a_ref, n2a_ref, n1b_ref, n2b_ref, sign_ref, o1_ref,
    e_ref, d_ref, sums_ref, acc_ref, keep_ref, send_ref,
):
    core = core_ref[0]
    rows = own_ref.shape[0]
    a, b = slice(0, rows), slice(rows, 2 * rows)
    chip = chip_rows(own_ref[...], both_ref[0:rows])
    near = jnp.concatenate([n2b_ref[...], n1b_ref[...], n2a_ref[...], n1a_ref[...]], axis=0)

    @pl.when(core == 0)
    def _():
        e_b = jnp.exp(gamma * rows_by_rows(chip[b], near))
        d_ba = jnp.exp(gamma * rows_by_rows(chip[b], chip[a]))
        sign = sign_ref[1]
        d_bb, pos, neg = signed_exp(sign, rows_by_rows(chip[b], chip[b]))
        neg_sum = over_columns(e_b) + over_columns(d_ba) + over_columns(neg)
        up, down, loss = factors(over_columns(pos), neg_sum)
        row_up = as_row(up)
        send_ref[rows : rows + 1, 0:rows] = over_rows(jnp.where(arrived_rows(o1_ref), loss, 0.0))
        coef = paired(sign, up, down, row_up, as_row(down), d_bb)
        total = jnp.dot(coef, chip[b], preferred_element_type=F32)
        total = total + scaled_dot(up, e_b, near) + scaled_dot(up, d_ba, chip[a])
        split_store(1, total, keep_ref, send_ref)

        d_ab = jnp.exp(gamma * rows_by_rows(chip[a], chip[b]))
        acc_ref[...] = scaled_dot(row_up, d_ab, chip[b])
        e_a = jnp.exp(gamma * rows_by_rows(chip[a], near))
        e_ref[a] = e_a
        d_aa, pos, neg = signed_exp(sign_ref[0], rows_by_rows(chip[a], chip[a]))
        d_ref[...] = d_aa
        sums_ref[:, 0:1] = over_columns(pos)
        sums_ref[:, 1:2] = over_columns(e_a) + over_columns(neg)

    @pl.when(core == 1)
    def _():
        scale = []
        for part, third, sign in ((a, near[b], sign_ref[0]), (b, both_ref[rows:], sign_ref[1])):
            anchors = near[part]
            e = jnp.exp(gamma * rows_by_rows(chip, anchors))
            e_ref[:, part] = e
            _, pos, neg = signed_exp(sign, rows_by_rows(anchors, anchors))
            others = jnp.exp(gamma * rows_by_rows(third, anchors))
            up, _, _ = factors(over_rows(pos), over_rows(e) + over_rows(neg) + over_rows(others))
            scale.append(up)
        scale = jnp.concatenate(scale, axis=1)
        split_store(0, scaled_dot(scale, e_ref[a], near), keep_ref, send_ref)
        acc_ref[...] = scaled_dot(scale, e_ref[b], near)


def late_kernel(
    core_ref, own_ref, both_ref, n1a_ref, n2a_ref, n1b_ref, n2b_ref, far_ref, sign_ref,
    e_ref, d_ref, sums_ref, acc_ref, o0_ref, keep_in, send_in, keep_ref, send_ref, loss_ref,
):
    core = core_ref[0]
    rows = own_ref.shape[0]
    a, b = slice(0, rows), slice(rows, 2 * rows)
    chip = chip_rows(own_ref[...], both_ref[0:rows])
    near = jnp.concatenate([n2b_ref[...], n1b_ref[...], n2a_ref[...], n1a_ref[...]], axis=0)
    far = far_ref[...]

    @pl.when(core == 0)
    def _():
        f = jnp.exp(gamma * rows_by_rows(chip[a], far))
        up, down, loss = factors(sums_ref[:, 0:1], sums_ref[:, 1:2] + over_columns(f))
        coef = paired(sign_ref[0], up, down, as_row(up), as_row(down), d_ref[...])
        total = acc_ref[...] + jnp.dot(coef, chip[a], preferred_element_type=F32)
        total = total + scaled_dot(up, e_ref[a], near) + scaled_dot(up, f, far)
        split_store(0, total, keep_ref, send_ref)
        loss_ref[...] = over_rows(jnp.where(arrived_rows(o0_ref), loss, 0.0))

    @pl.when(core == 1)
    def _():
        f = jnp.exp(gamma * rows_by_rows(chip[b], far))
        _, pos, neg = signed_exp(sign_ref[2], rows_by_rows(far, far))
        others = jnp.exp(gamma * rows_by_rows(near, far))
        up, _, _ = factors(over_rows(pos), over_rows(f) + over_rows(neg) + over_rows(others))
        split_store(1, acc_ref[...] + scaled_dot(up, f, far), keep_ref, send_ref)
        loss_ref[...] = jnp.zeros_like(loss_ref)


def final_kernel(core_ref, x_ref, keep_ref, other_ref, losses_ref, grad_ref, loss_ref):
    rows = keep_ref.shape[0]
    loss_ref[...] = jnp.where(
        core_ref[0] == 0, losses_ref[...], other_ref[rows : rows + 1, 0:rows]
    )
    features = x_ref.shape[-1]
    half = keep_ref.shape[0] // 2
    for which in range(2):
        part = slice(which * half, (which + 1) * half)
        total = keep_ref[part] + other_ref[part]
        x = x_ref[:, which].astype(F32).reshape(half, features)
        inv = lax.rsqrt(jnp.sum(x * x, axis=1, keepdims=True) + 1e-06)
        u = x * inv
        grad = (total - u * jnp.sum(u * total, axis=1, keepdims=True)) * inv
        grad_ref[:, which] = grad.reshape(half // 8, 8, features).astype(BF16)


def copy_kernel(x_ref, out_ref):
    out_ref[...] = x_ref[...]


VMEM = pl.BlockSpec(memory_space=pltpu.VMEM)
SMEM = pl.BlockSpec(memory_space=pltpu.SMEM)


def shape(*size, dtype=F32):
    return jax.ShapeDtypeStruct(size, dtype)


def call(kernel, inputs, outputs, work, aliases=None):
    return pl.pallas_call(
        kernel,
        out_shape=outputs,
        in_specs=[SMEM if a.ndim == 1 else VMEM for a in inputs],
        out_specs=jax.tree.map(lambda _: VMEM, outputs),
        input_output_aliases=aliases or {},
        compiler_params=pltpu.CompilerParams(vmem_limit_bytes=LIMIT),
        cost_estimate=pl.CostEstimate(
            flops=int(work * 10**9), bytes_accessed=10**5, transcendentals=0
        ),
    )(*inputs)


def on_device(embeddings, order):
    rows, features = embeddings.shape
    peers = lax.axis_size(WHERE)
    per_peer = rows // peers
    half = rows // 2
    core = lax.axis_index("c").astype(jnp.int32).reshape(1)
    ring = lax.axis_size("y")

    def fetch_order(moves):
        route = [
            ((c * ring + y) * 2 + h, (core * ring + (y + s) % ring) * 2 + c)
            for h, core, s in moves
            for c in range(2)
            for y in range(ring)
        ]
        return lax.ppermute(order, ("c", "y", "zh"), route)

    def along(value, moves):
        route = [(a * ring + y, b * ring + (y + s) % ring) for a, b, s in moves for y in range(ring)]
        return lax.ppermute(value, ("c", "y"), route)

    o0 = fetch_order(((0, 0, 0), (1, 1, -1)))
    o1 = fetch_order(((1, 0, 0), (0, 1, -1)))
    o2 = fetch_order(((0, 1, -2),))
    arrived = lax.all_to_all(
        embeddings.reshape(peers, per_peer, features), WHERE, 0, 0, tiled=True
    ).reshape(peers // 2, 2, per_peer, features)
    block = shape(rows, features, dtype=BF16)
    half_block = shape(half, features, dtype=BF16)

    own, one, two = call(pack_kernel, (core, arrived), (block, half_block, half_block), 0.01)
    straight = ((0, 0, 1), (1, 1, -1))
    across = ((1, 0, 1), (0, 1, -1))
    n1a = along(one, straight)
    n2a = along(two, across)
    n1b = along(two, straight)
    n2b = along(one, across)
    near = (n1a, n2a, n1b, n2b)
    relay, both = call(
        relay_kernel, (own, n1a, n2a), (block, shape(2 * rows, features, dtype=BF16)), 0.01
    )
    far = along(relay, straight)
    sib = along(both, ((0, 1, 0), (1, 0, 0)))

    sign = call(classes_kernel, (core, o0, o1, o2), shape(3, rows, rows), 0.5)
    half_grads = (shape(rows, features), shape(rows + 8, features))
    e, d, sums, acc, keep, send = call(
        early_kernel,
        (core, own, sib, *near, sign, o1),
        (
            shape(2 * rows, 2 * rows),
            shape(rows, rows),
            shape(rows, 8),
            shape(rows, features),
            *half_grads,
        ),
        2.0,
    )
    keep, send, losses = call(
        late_kernel,
        (core, own, sib, *near, far, sign, e, d, sums, acc, o0, keep, send),
        (*half_grads, shape(1, rows)),
        0.8,
        {14: 0, 15: 1},
    )
    other = along(send, ((0, 1, 0), (1, 0, 0)))
    grad, loss = call(
        final_kernel,
        (core, arrived, keep, other, losses),
        (shape(peers // 2, 2, per_peer, features, dtype=BF16), shape(1, rows)),
        0.01,
    )
    row_loss = lax.ppermute(
        loss, ("c", "zh"), [(c * 2 + h, h * 2 + c) for h in range(2) for c in range(2)]
    )
    row_loss = call(copy_kernel, (row_loss,), shape(1, rows), 0.001)
    sent_back = lax.all_to_all(
        grad.reshape(peers, per_peer, features), WHERE, 0, 0, tiled=True
    )
    return sent_back.reshape(rows, features), row_loss


def solution(mesh):
    dp, grp = mesh.devices.shape
    parts = Mesh(
        mesh.devices.reshape(dp // 8, 4, 2, grp // 2, 2), ("zl", "x", "c", "y", "zh")
    )
    placed = P(("zl", "x", "c", "y", "zh"), None)

    def step(embeddings, order):
        return on_device(embeddings, order)

    step = jax.shard_map(
        step, mesh=parts, in_specs=(placed, placed), out_specs=(placed, placed), check_vma=False
    )
    return step
```

```python
import jax
import jax.numpy as jnp
from jax import lax
from jax.experimental import pallas as pl
from jax.experimental.pallas import tpu as pltpu
from jax.sharding import Mesh
from jax.sharding import PartitionSpec as P


K = 16
gamma = 16.0
F32 = jnp.float32
BF16 = jnp.bfloat16
WHERE = ("zl", "x", "zh")
LIMIT = 20 * 2**20


def rows_by_rows(a, b):
    return lax.dot_general(a, b, (((1,), (1,)), ((), ())), preferred_element_type=F32)


def chip_rows(own, sib):
    half = own.shape[0] // 2
    return jnp.concatenate([own[0:half], sib[0:half], own[half:], sib[half:]], axis=0)


def cols_by_cols(a, b):
    return lax.dot_general(a, b, (((0,), (0,)), ((), ())), preferred_element_type=F32)


def as_row(column):
    return jnp.broadcast_to(column, (column.shape[0], 128)).T[0:1]


def over_rows(value):
    return jnp.sum(value, axis=0, keepdims=True)


def over_columns(value):
    return jnp.sum(value, axis=1, keepdims=True)


def arrived_rows(order_ref):
    rows = order_ref.shape[1]
    half = rows // 2
    i = lax.broadcasted_iota(jnp.int32, (rows, rows), 0)
    source = jnp.where(i < half, 0, 1)
    i = i - source * half
    return (i // 8) * 16 + source * 8 + i % 8 == order_ref[...]


def classes_kernel(core_ref, o0_ref, o1_ref, o2_ref, sign_ref):
    core = core_ref[0]
    rows = o0_ref.shape[1]
    slot = lax.broadcasted_iota(jnp.int32, (rows, 128), 0) // K
    table = jnp.where(lax.broadcasted_iota(jnp.int32, (rows, 128), 1) == slot, 1.0, 0.0)
    table = table.astype(BF16)
    diagonal = lax.broadcasted_iota(jnp.int32, (rows, rows), 0) == lax.broadcasted_iota(
        jnp.int32, (rows, rows), 1
    )

    def fill(b, ref):
        chosen = jnp.where(arrived_rows(ref), 1.0, 0.0).astype(BF16)
        hot = jnp.dot(chosen, table, preferred_element_type=F32).astype(BF16)
        sign_ref[b] = jnp.where(diagonal, 0.0, 1.0 - 2.0 * rows_by_rows(hot, hot))

    fill(0, o0_ref)
    fill(1, o1_ref)

    @pl.when(core == 1)
    def _():
        fill(2, o2_ref)


def pack_kernel(core_ref, x_ref, full_ref, one_ref, two_ref):
    core = core_ref[0]
    half = one_ref.shape[0]
    for which in range(2):
        x = x_ref[:, which].astype(F32).reshape(half, x_ref.shape[-1])
        inv = lax.rsqrt(jnp.sum(x * x, axis=1, keepdims=True) + 1e-06)
        unit = (x * inv).astype(BF16)
        full_ref[which * half : (which + 1) * half] = unit

        @pl.when(core == 1 - which)
        def _():
            one_ref[...] = unit

        @pl.when(core == which)
        def _():
            two_ref[...] = unit


def relay_kernel(own_ref, n1a_ref, n2a_ref, out_ref, both_ref):
    half = n1a_ref.shape[0]
    rows = 2 * half
    out_ref[0:half] = n2a_ref[...]
    out_ref[half:] = n1a_ref[...]
    both_ref[0:rows] = own_ref[...]
    both_ref[rows : rows + half] = n2a_ref[...]
    both_ref[rows + half :] = n1a_ref[...]


def signed_exp(sign, sim):
    e = jnp.exp(gamma * sign * sim)
    return e, jnp.where(sign < 0.0, e, 0.0), jnp.where(sign > 0.0, e, 0.0)


def factors(pos_sum, neg_sum):
    product = pos_sum * neg_sum
    weight = product / (1.0 + product)
    return gamma * weight / neg_sum, gamma * weight / pos_sum, jnp.log(1.0 + product)


def scaled_dot(scale, e, rows):
    return jnp.dot((scale * e).astype(BF16), rows, preferred_element_type=F32)


def paired(sign, up, down, row_up, row_down, e):
    scale = jnp.where(sign < 0.0, -(down + row_down), 0.0)
    return (jnp.where(sign > 0.0, up + row_up, scale) * e).astype(BF16)


def split_store(b, total, keep_ref, send_ref):
    half = total.shape[0] // 2
    keep_ref[b * half : (b + 1) * half] = total[0:half]
    send_ref[b * half : (b + 1) * half] = total[half:]


def early_kernel(
    core_ref, own_ref, both_ref, n1a_ref, n2a_ref, n1b_ref, n2b_ref, sign_ref, o1_ref,
    e_ref, d_ref, sums_ref, acc_ref, keep_ref, send_ref,
):
    core = core_ref[0]
    rows = own_ref.shape[0]
    a, b = slice(0, rows), slice(rows, 2 * rows)
    chip = chip_rows(own_ref[...], both_ref[0:rows])
    near = jnp.concatenate([n2b_ref[...], n1b_ref[...], n2a_ref[...], n1a_ref[...]], axis=0)

    @pl.when(core == 0)
    def _():
        e_b = jnp.exp(gamma * rows_by_rows(chip[b], near))
        d_ba = jnp.exp(gamma * rows_by_rows(chip[b], chip[a]))
        sign = sign_ref[1]
        d_bb, pos, neg = signed_exp(sign, rows_by_rows(chip[b], chip[b]))
        neg_sum = over_columns(e_b) + over_columns(d_ba) + over_columns(neg)
        up, down, loss = factors(over_columns(pos), neg_sum)
        send_ref[rows : rows + 1, 0:rows] = over_rows(jnp.where(arrived_rows(o1_ref), loss, 0.0))
        coef = paired(sign, up, down, as_row(up), as_row(down), d_bb)
        total = jnp.dot(coef, chip[b], preferred_element_type=F32)
        coef_ba = (up * d_ba).astype(BF16)
        acc_ref[...] = cols_by_cols(coef_ba, chip[b])
        total = total + jnp.dot(coef_ba, chip[a], preferred_element_type=F32)
        total = total + scaled_dot(up, e_b, near)
        split_store(1, total, keep_ref, send_ref)
        e_a = jnp.exp(gamma * rows_by_rows(chip[a], near))
        e_ref[a] = e_a
        d_aa, pos, neg = signed_exp(sign_ref[0], rows_by_rows(chip[a], chip[a]))
        d_ref[...] = d_aa
        sums_ref[:, 0:1] = over_columns(pos)
        sums_ref[:, 1:2] = over_columns(e_a) + over_columns(neg)

    @pl.when(core == 1)
    def _():
        scale = []
        for part, third, sign in ((a, near[b], sign_ref[0]), (b, both_ref[rows:], sign_ref[1])):
            anchors = near[part]
            e = jnp.exp(gamma * rows_by_rows(chip, anchors))
            e_ref[:, part] = e
            _, pos, neg = signed_exp(sign, rows_by_rows(anchors, anchors))
            others = jnp.exp(gamma * rows_by_rows(third, anchors))
            up, _, _ = factors(over_rows(pos), over_rows(e) + over_rows(neg) + over_rows(others))
            scale.append(up)
        scale = jnp.concatenate(scale, axis=1)
        split_store(0, scaled_dot(scale, e_ref[a], near), keep_ref, send_ref)
        acc_ref[...] = scaled_dot(scale, e_ref[b], near)


def late_kernel(
    core_ref, own_ref, both_ref, n1a_ref, n2a_ref, n1b_ref, n2b_ref, far_ref, sign_ref,
    e_ref, d_ref, sums_ref, acc_ref, keep_in, send_in, keep_ref, send_ref, loss_ref,
):
    core = core_ref[0]
    rows = own_ref.shape[0]
    a, b = slice(0, rows), slice(rows, 2 * rows)
    chip = chip_rows(own_ref[...], both_ref[0:rows])
    near = jnp.concatenate([n2b_ref[...], n1b_ref[...], n2a_ref[...], n1a_ref[...]], axis=0)
    far = far_ref[...]

    @pl.when(core == 0)
    def _():
        f = jnp.exp(gamma * rows_by_rows(chip[a], far))
        up, down, loss = factors(sums_ref[:, 0:1], sums_ref[:, 1:2] + over_columns(f))
        coef = paired(sign_ref[0], up, down, as_row(up), as_row(down), d_ref[...])
        total = acc_ref[...] + jnp.dot(coef, chip[a], preferred_element_type=F32)
        total = total + scaled_dot(up, e_ref[a], near) + scaled_dot(up, f, far)
        split_store(0, total, keep_ref, send_ref)
        loss_ref[:, 0:1] = loss

    @pl.when(core == 1)
    def _():
        f = jnp.exp(gamma * rows_by_rows(chip[b], far))
        _, pos, neg = signed_exp(sign_ref[2], rows_by_rows(far, far))
        others = jnp.exp(gamma * rows_by_rows(near, far))
        up, _, _ = factors(over_rows(pos), over_rows(f) + over_rows(neg) + over_rows(others))
        split_store(1, acc_ref[...] + scaled_dot(up, f, far), keep_ref, send_ref)


def prepare_kernel(core_ref, x_ref, loss_col_ref, o0_ref, u_ref, inv_ref, loss_ref):
    features = x_ref.shape[-1]
    half = u_ref.shape[0] // 2
    for which in range(2):
        part = slice(which * half, (which + 1) * half)
        x = x_ref[:, which].astype(F32).reshape(half, features)
        inv = lax.rsqrt(jnp.sum(x * x, axis=1, keepdims=True) + 1e-06)
        u_ref[part] = x * inv
        inv_ref[part, 0:1] = inv

    @pl.when(core_ref[0] == 0)
    def _():
        loss_ref[...] = over_rows(jnp.where(arrived_rows(o0_ref), loss_col_ref[:, 0:1], 0.0))


def final_kernel(core_ref, u_ref, inv_ref, keep_ref, other_ref, losses_ref, grad_ref, loss_ref):
    rows, features = keep_ref.shape
    loss_ref[...] = jnp.where(
        core_ref[0] == 0, losses_ref[...], other_ref[rows : rows + 1, 0:rows]
    )
    half = rows // 2
    for which in range(2):
        part = slice(which * half, (which + 1) * half)
        total = keep_ref[part] + other_ref[part]
        u = u_ref[part]
        grad = (total - u * jnp.sum(u * total, axis=1, keepdims=True)) * inv_ref[part, 0:1]
        grad_ref[:, which] = grad.reshape(half // 8, 8, features).astype(BF16)


def copy_kernel(x_ref, out_ref):
    out_ref[...] = x_ref[...]


VMEM = pl.BlockSpec(memory_space=pltpu.VMEM)
SMEM = pl.BlockSpec(memory_space=pltpu.SMEM)


def shape(*size, dtype=F32):
    return jax.ShapeDtypeStruct(size, dtype)


def call(kernel, inputs, outputs, work, aliases=None):
    return pl.pallas_call(
        kernel,
        out_shape=outputs,
        in_specs=[SMEM if a.ndim == 1 else VMEM for a in inputs],
        out_specs=jax.tree.map(lambda _: VMEM, outputs),
        input_output_aliases=aliases or {},
        compiler_params=pltpu.CompilerParams(vmem_limit_bytes=LIMIT),
        cost_estimate=pl.CostEstimate(
            flops=int(work * 10**9), bytes_accessed=10**5, transcendentals=0
        ),
    )(*inputs)


def on_device(embeddings, order):
    rows, features = embeddings.shape
    peers = lax.axis_size(WHERE)
    per_peer = rows // peers
    half = rows // 2
    core = lax.axis_index("c").astype(jnp.int32).reshape(1)
    ring = lax.axis_size("y")

    def fetch_order(moves):
        route = [
            ((c * ring + y) * 2 + h, (core * ring + (y + s) % ring) * 2 + c)
            for h, core, s in moves
            for c in range(2)
            for y in range(ring)
        ]
        return lax.ppermute(order, ("c", "y", "zh"), route)

    def along(value, moves):
        route = [(a * ring + y, b * ring + (y + s) % ring) for a, b, s in moves for y in range(ring)]
        return lax.ppermute(value, ("c", "y"), route)

    o0 = fetch_order(((0, 0, 0), (1, 1, -1)))
    o1 = fetch_order(((1, 0, 0), (0, 1, -1)))
    o2 = fetch_order(((0, 1, -2),))
    arrived = lax.all_to_all(
        embeddings.reshape(peers, per_peer, features), WHERE, 0, 0, tiled=True
    ).reshape(peers // 2, 2, per_peer, features)
    block = shape(rows, features, dtype=BF16)
    half_block = shape(half, features, dtype=BF16)

    own, one, two = call(pack_kernel, (core, arrived), (block, half_block, half_block), 0.01)
    straight = ((0, 0, 1), (1, 1, -1))
    across = ((1, 0, 1), (0, 1, -1))
    n1a = along(one, straight)
    n2a = along(two, across)
    n1b = along(two, straight)
    n2b = along(one, across)
    near = (n1a, n2a, n1b, n2b)
    relay, both = call(
        relay_kernel, (own, n1a, n2a), (block, shape(2 * rows, features, dtype=BF16)), 0.01
    )
    far = along(relay, straight)
    sib = along(both, ((0, 1, 0), (1, 0, 0)))

    sign = call(classes_kernel, (core, o0, o1, o2), shape(3, rows, rows), 0.5)
    half_grads = (shape(rows, features), shape(rows + 8, features))
    e, d, sums, acc, keep, send = call(
        early_kernel,
        (core, own, sib, *near, sign, o1),
        (
            shape(2 * rows, 2 * rows),
            shape(rows, rows),
            shape(rows, 8),
            shape(rows, features),
            *half_grads,
        ),
        2.0,
    )
    keep, send, loss_col = call(
        late_kernel,
        (core, own, sib, *near, far, sign, e, d, sums, acc, keep, send),
        (*half_grads, shape(rows, 8)),
        0.8,
        {13: 0, 14: 1},
    )
    other = along(send, ((0, 1, 0), (1, 0, 0)))
    u, inv, losses = call(
        prepare_kernel,
        (core, arrived, loss_col, o0),
        (shape(rows, features), shape(rows, 8), shape(1, rows)),
        0.01,
    )
    grad, loss = call(
        final_kernel,
        (core, u, inv, keep, other, losses),
        (shape(peers // 2, 2, per_peer, features, dtype=BF16), shape(1, rows)),
        0.01,
    )
    row_loss = lax.ppermute(
        loss, ("c", "zh"), [(c * 2 + h, h * 2 + c) for h in range(2) for c in range(2)]
    )
    row_loss = call(copy_kernel, (row_loss,), shape(1, rows), 0.001)
    sent_back = lax.all_to_all(
        grad.reshape(peers, per_peer, features), WHERE, 0, 0, tiled=True
    )
    return sent_back.reshape(rows, features), row_loss


def solution(mesh):
    dp, grp = mesh.devices.shape
    parts = Mesh(
        mesh.devices.reshape(dp // 8, 4, 2, grp // 2, 2), ("zl", "x", "c", "y", "zh")
    )
    placed = P(("zl", "x", "c", "y", "zh"), None)

    def step(embeddings, order):
        return on_device(embeddings, order)

    step = jax.shard_map(
        step, mesh=parts, in_specs=(placed, placed), out_specs=(placed, placed), check_vma=False
    )
    return step
```
